256 devices in a mesh: seq: 8 (over z_lo, y), outer: 8 (over x, core), inner: 4 (over z_hi).
Axes of the slice: x: 4, y: 4, z: 8 (z_hi: 4, z_lo: 2; z = z_hi * 2 + z_lo), core: 2. Of those that a mesh axis runs over, the one named last changes fastest.
Arguments:
- tokens: bfloat16 [32768, 4096], P(('seq', 'outer', 'inner')), parts along dimension 0, may hold values from -6 to 6
- att_ids: int32 [32768, 2, 2], P(('seq', 'outer', 'inner')), parts along dimension 0, may hold values from 0 to 3, all different within a row
- mlp_ids: int32 [32768, 8], P(('seq', 'outer', 'inner')), parts along dimension 0, may hold values from 0 to 63, all different within a row; in each aligned block of 128 rows (0 to 127, 128 to 255, ...) at most 20 rows name the same one
- att_gain: float32 [4096], replicated, may hold values from 0.25 to 1.75
- att_in: bfloat16 [4096, 768], P('inner'), may hold values from -16 to 16
- att_router: bfloat16 [4096, 8], P('inner'), may hold values from -0.09375 to 0.09375
- att_out: bfloat16 [512, 4096], P(None, 'inner'), may hold values from -0.75 to 0.75
- mlp_gain: float32 [4096], replicated, may hold values from 0.25 to 1.75
- mlp_router: bfloat16 [4096, 64], replicated, may hold values from -0.09375 to 0.09375
- w_up: bfloat16 [64, 4096, 256], P(('outer', 'inner')), may hold values from -0.09375 to 0.09375
- w_down: bfloat16 [64, 256, 4096], P(('outer', 'inner')), may hold values from -0.375 to 0.375
Outputs:
- layer_out: bfloat16 [32768, 4096], P(('seq', 'outer', 'inner')), parts along dimension 0
The draws below stay inside these ranges and needn't reach their ends.
There are 8 independent parts, one for each index of `seq`. The reference program is written for one: setup_inputs(seed, part) draws one part's arguments, and reference() takes and returns one part's arrays. A program takes and returns all parts, laid end to end along the dimension named above; an argument that names none is the same for every part. Nothing has to cross between parts.
Inputs may be any that keep to these rules, and one draw needn't show every extreme that they name: `att_ids`: the 2 ids of one token and head differ. `mlp_ids`: among the rows of one device each expert is named at most 20 times, a bound that some block reaches in some devices' rows.
All inputs are finite; a program needn't handle non-finite values.
Results may differ from the reference program's by a relative error of at most 0.008.
Values may be sent and summed in bfloat16 or wider, within the bound.
A program may use at most 128 MiB of HBM per device.

```python
import math
import jax
import jax.numpy as jnp
import numpy as np
from jax import lax

D = 4096
HEADS = 2
HDIM = 64
ATT_EXP = 4
ATT_TOP = 2
MLP_HID = 256
MLP_TOP = 8
TOK_DEV = 128
EXPERTS = 64
CAP = 20
TOKENS = 4096
N_OUTER = 8
N_INNER = 4


def draw_att_in(key, part):
    columns = 2 * HEADS * HDIM + HEADS * ATT_EXP * HDIM
    weights = jax.random.normal(jax.random.fold_in(key, 11), (D, columns), jnp.float32) * D ** (-0.5)
    return weights.astype(jnp.bfloat16)


def steps_of(own_key, shape, shards, smallest, high):
    loudness = 1.0
    for dim, shards_of in shards:
        draws = jax.random.uniform(jax.random.fold_in(jax.random.fold_in(own_key, 6), dim), (shards_of,), jnp.float32, smallest / len(shards), high / len(shards))
        loudness = loudness * jnp.repeat(jnp.exp(draws), shape[dim] // shards_of).reshape((-1,) + (1,) * (len(shape) - 1 - dim))
    return loudness


def distinct(key, rows, number_of, top, lift):
    ranking = jax.random.permutation(jax.random.fold_in(key, 1), number_of)
    pull = ranking
    for power in range(3):
        pull = pull * pull // number_of
    pull = pull * lift // number_of
    chance = jax.random.randint(jax.random.fold_in(key, 2), (rows, number_of), 0, 4096) + pull
    holders = jax.random.permutation(jax.random.fold_in(key, 3), rows)[jnp.arange(number_of) % rows]
    chance = jnp.where(jnp.arange(rows)[:, None] == holders[None, :], 1 << 14, chance)
    merit = chance * number_of + jnp.arange(number_of)
    return lax.top_k(merit.astype(jnp.int32), top)[1].astype(jnp.int32)


def routed_block(stream_key, own, number, rows, number_of, top, most, skew):
    sequence = jax.random.permutation(stream_key, number_of)
    heavy_load, ordinary = portions_of(number_of, rows * top, most, skew, True), portions_of(number_of, rows * top, most, skew, False)
    places = jnp.arange(number_of)

    def named(lengths, rotation):
        used = int((lengths > 0).sum())
        fixed = max(1, used // 4)
        shifted = fixed + (places - fixed + rotation * (used - fixed)) % max(1, number_of - fixed)
        return jnp.zeros((number_of,), jnp.int32).at[sequence[jnp.where(places < fixed, places, shifted)]].set(jnp.asarray(lengths, jnp.int32))

    lengths = jnp.where(number % 4 == 0, named(heavy_load, number // 4), named(ordinary, number - number // 4 - 1))
    mixed = jax.random.permutation(jax.random.fold_in(own, 3), number_of)
    donor, sink = mixed[0:number_of // 2 * 2:2], mixed[1:number_of // 2 * 2:2]
    room = jnp.minimum(lengths[donor] - 1, most - lengths[sink]) // 2
    room = jnp.where((donor == sequence[0]) | (sink == sequence[0]) | (lengths[sink] == 0), 0, jnp.maximum(room, 0))
    shifted = jax.random.randint(jax.random.fold_in(own, 4), (number_of // 2,), 0, 1 << 20) % (room + 1)
    lengths = lengths.at[donor].add(-shifted).at[sink].add(shifted)
    items = jnp.searchsorted(jnp.cumsum(lengths), jnp.arange(rows * top), side="right").astype(jnp.int32)
    listing = items.reshape(top, rows).T
    listing = listing[jax.random.permutation(jax.random.fold_in(own, 1), rows)]
    rotation = jax.random.randint(jax.random.fold_in(own, 2), (rows, 1), 0, top)
    return jnp.take_along_axis(listing, (jnp.arange(top)[None, :] + rotation) % top, axis=1)


def portions_of(amount, total, reach, skew, full):
    loads = [(1 << 20) // math.isqrt(rank ** skew) + 1 for rank in range(1, amount + 1)]
    largest = reach if full else min(reach, max(-(-total // amount), total * loads[0] // sum(loads)))
    least = 1 if total - largest >= amount - 1 else 0
    given, rest = [largest] + [least] * (amount - 1), total - largest - least * (amount - 1)
    while rest > 0:
        movable = [i for i in range(1, amount) if given[i] < largest] or [i for i in range(1, amount) if given[i] < reach]
        whole, remaining = sum([loads[i] for i in movable]), rest
        for i in movable:
            more = min(reach - given[i], max(1, remaining * loads[i] // whole), rest)
            given[i] = given[i] + more
            rest = rest - more
    return np.array(given)


def scatter_about(rng, shape, scale, bound, pieces=(), kind=jnp.bfloat16):
    entries = jax.random.normal(rng, shape, jnp.float32) * scale
    if len(pieces) > 0:
        entries = steps_of(rng, shape, pieces, -0.22, 0.18) * entries
    return jnp.clip(entries, min=-bound, max=bound).astype(kind)


def setup_inputs(seed: int = 0, part: int = 0) -> dict:
    streams_of = jax.random.split(jax.random.key(seed), 12)
    part_keys = jax.random.split(jax.random.fold_in(streams_of[11], part), 12)
    tokens = scatter_about(part_keys[0], (TOKENS, D), 1.0, 6.0, ((0, 32),))
    att_ids = distinct(part_keys[1], TOKENS * HEADS, ATT_EXP, ATT_TOP, 4096).reshape((TOKENS, HEADS, ATT_TOP))
    mlp_ids_keys = jax.random.split(jax.random.fold_in(part_keys[2], 1), TOKENS // TOK_DEV)
    mlp_ids_turns = jax.random.permutation(jax.random.fold_in(part_keys[2], 3), TOKENS // TOK_DEV)
    mlp_ids = jax.vmap(lambda own, number: routed_block(jax.random.fold_in(part_keys[2], 2), own, number, TOK_DEV, EXPERTS, MLP_TOP, CAP, 2))(mlp_ids_keys, mlp_ids_turns).reshape((TOKENS, MLP_TOP))
    att_gain = jnp.clip(1.0 + 0.15 * jax.random.normal(streams_of[3], (D,), jnp.float32), 0.25, 1.75)
    att_in = draw_att_in(jax.random.fold_in(streams_of[11], 71), part)
    att_router = scatter_about(streams_of[5], (D, HEADS * ATT_EXP), D ** -0.5, 0.09375, ((0, 4),))
    att_out = scatter_about(streams_of[6], (HEADS * ATT_EXP * HDIM, D), (HEADS * HDIM // 2) ** -0.5, 0.75, ((1, 4),))
    mlp_gain = jnp.clip(1.0 + 0.15 * jax.random.normal(streams_of[7], (D,), jnp.float32), 0.25, 1.75)
    mlp_router = scatter_about(streams_of[8], (D, EXPERTS), D ** -0.5, 0.09375)
    w_up = scatter_about(streams_of[9], (EXPERTS, D, MLP_HID), D ** -0.5, 0.09375, ((0, 32),))
    w_down = scatter_about(streams_of[10], (EXPERTS, MLP_HID, D), MLP_HID ** -0.5, 0.375, ((0, 32),))
    return dict(tokens=tokens, att_ids=att_ids, mlp_ids=mlp_ids, att_gain=att_gain, att_in=att_in, att_router=att_router, att_out=att_out, mlp_gain=mlp_gain, mlp_router=mlp_router, w_up=w_up, w_down=w_down)


epsilon = 1e-05

def rms_norm(values_in, gain_vector):
    floats = values_in.astype(jnp.float32)
    return floats * lax.rsqrt(lax.optimization_barrier(jnp.mean(floats * floats, axis=-1, keepdims=True)) + epsilon) * gain_vector

def reference(tokens, att_ids, mlp_ids, att_gain, att_in, att_router, att_out, mlp_gain, mlp_router, w_up, w_down):
    normed = rms_norm(tokens, att_gain).astype(jnp.bfloat16)
    proj = jnp.dot(normed, att_in, preferred_element_type=jnp.float32)
    head_width = HEADS * HDIM
    query = proj[:, :head_width].astype(jnp.bfloat16).reshape(TOKENS, HEADS, HDIM)
    keys = proj[:, head_width:2 * head_width].astype(jnp.bfloat16).reshape(TOKENS, HEADS, HDIM)
    value_all = proj[:, 2 * head_width:].reshape(TOKENS, HEADS, ATT_EXP, HDIM)
    att_logit = jnp.dot(normed, att_router, preferred_element_type=jnp.float32).reshape(TOKENS, HEADS, ATT_EXP)
    chosen = lax.optimization_barrier(jnp.sum((att_ids[..., None] == jnp.arange(ATT_EXP)[None, None, None, :]).astype(jnp.float32), axis=2))
    att_weight = jax.nn.sigmoid(att_logit) * chosen
    values = lax.optimization_barrier(jnp.sum(att_weight[..., None] * value_all, axis=2)).astype(jnp.bfloat16)
    scores = jnp.einsum('thd,shd->hts', query.astype(jnp.float32), keys.astype(jnp.float32), precision=lax.Precision.HIGHEST) * HDIM ** (-0.5)
    position = jnp.arange(TOKENS)
    causal = position[None, :] <= position[:, None]
    scores = jnp.where(causal[None], scores, -1e+30)
    probabilities = jax.nn.softmax(scores, axis=-1)
    attended = jnp.einsum('hts,shd->thd', probabilities, values.astype(jnp.float32), precision=lax.Precision.HIGHEST)
    head_normed = attended * lax.rsqrt(lax.optimization_barrier(jnp.mean(attended * attended, axis=-1, keepdims=True)) + epsilon)
    mixed = (head_normed[:, :, None, :] * att_weight[..., None]).reshape(TOKENS, HEADS * ATT_EXP * HDIM)
    mixed = mixed.astype(jnp.bfloat16)
    hidden_state = tokens.astype(jnp.float32) + jnp.dot(mixed, att_out, preferred_element_type=jnp.float32)
    mlp_in = rms_norm(hidden_state, mlp_gain).astype(jnp.bfloat16)
    logits = jnp.dot(mlp_in, mlp_router, preferred_element_type=jnp.float32)
    picked = (mlp_ids[..., None] == jnp.arange(EXPERTS)[None, None, :]).astype(jnp.float32)
    gates = jax.nn.sigmoid(lax.optimization_barrier(jnp.sum(picked * logits[:, None, :], axis=-1)))
    flat_ids = mlp_ids.reshape(-1)
    flat_gates = gates.reshape(-1)
    assignments = TOKENS * MLP_TOP
    slot_count = N_OUTER * N_INNER * CAP

    def one_expert(expert, accumulated):
        positions = jnp.nonzero(flat_ids == expert, size=slot_count, fill_value=assignments)[0].astype(jnp.int32)
        valid = (positions < assignments).astype(jnp.float32)
        clipped = jnp.minimum(positions, assignments - 1).astype(jnp.int32)
        token_index = (clipped // MLP_TOP).astype(jnp.int32)
        inputs = mlp_in[token_index]
        hidden = jnp.maximum(jnp.dot(inputs, w_up[expert], preferred_element_type=jnp.float32), 0.0)
        hidden = hidden.astype(jnp.bfloat16)
        result = jnp.dot(hidden, w_down[expert], preferred_element_type=jnp.float32).astype(jnp.bfloat16)
        weighted = (flat_gates[clipped] * valid)[:, None] * result.astype(jnp.float32)
        return accumulated.at[token_index].add(weighted)
    mlp_out = lax.fori_loop(0, EXPERTS, one_expert, jnp.zeros((TOKENS, D), jnp.float32))
    return (hidden_state + mlp_out).astype(jnp.bfloat16)
```

```python
import functools

import jax
import jax.numpy as jnp
from jax import lax
from jax.experimental import pallas as pl
from jax.experimental.pallas import tpu as pltpu
from jax.sharding import PartitionSpec as P

D = 4096
HEADS = 2
HDIM = 64
ATT_EXP = 4
EXT = D + 128
ROWS = 128
epsilon = 1e-05
MESH = pl.DeviceIdType.MESH
ANY = pl.BlockSpec(memory_space=pl.ANY)
VM = pl.BlockSpec(memory_space=pltpu.VMEM)
DMA = pltpu.SemaphoreType.DMA
BF = jnp.bfloat16
F32 = jnp.float32


def rms_norm(values_in, gain_vector):
    floats = values_in.astype(F32)
    return (
        floats
        * lax.rsqrt(jnp.mean(floats * floats, axis=-1, keepdims=True) + epsilon)
        * gain_vector
    )


class Place:
    def __init__(self):
        self.seq, self.outer, self.inner = (lax.axis_index(a) for a in ("seq", "outer", "inner"))
        self.zl, self.y = self.seq // 4, self.seq % 4
        self.x, self.c = self.outer // 2, self.outer % 2

    def along_z(self, d):
        return (self.seq, self.outer, (self.inner + d) % 4)

    def along_y(self, d):
        return (self.zl * 4 + (self.y + d) % 4, self.outer, self.inner)

    def along_x(self, d):
        return (self.seq, ((self.x + d) % 4) * 2 + self.c, self.inner)

    def sibling(self):
        return (self.seq, self.x * 2 + 1 - self.c, self.inner)

    def pair(self):
        return ((1 - self.zl) * 4 + self.y, self.outer, self.inner)

    def beyond(self):
        return ((1 - self.zl) * 4 + self.y, self.outer, (self.inner + 2 * self.zl - 1) % 4)


def meet(peers):
    barrier = pltpu.get_barrier_semaphore()
    for peer in peers:
        pl.semaphore_signal(barrier, inc=1, device_id=peer, device_id_type=MESH)
    pl.semaphore_wait(barrier, len(peers))


def remote(src, dst, send, recv, peer):
    return pltpu.make_async_remote_copy(
        src_ref=src, dst_ref=dst, send_sem=send, recv_sem=recv, device_id=peer, device_id_type=MESH
    )


def spread_over_z(at, own, gathered, full, p, sems):
    s1, r1, s2, r2, s3, r3 = sems
    n = full // 16
    spans = (
        pl.ds(pl.multiple_of(p.c * (4 * n) + p.y * n, n), n),
        pl.ds(pl.multiple_of(8 * n + p.c * (4 * n) + p.x * n, n), n),
    )
    halves = tuple(pl.ds(pl.multiple_of(8 * n * h + p.c * (4 * n), 4 * n), 4 * n) for h in range(2))

    def first(d, h):
        return remote(
            own.at[spans[h]], gathered.at[p.inner, spans[h]], s1.at[at, d - 1, h], r1.at[at, d - 1, h], p.along_z(d)
        )

    def second(d, h, e):
        j = (p.inner - d + 4) % 4
        peer = p.along_y(e) if h == 0 else p.along_x(e)
        block = gathered.at[j, spans[h]]
        return remote(block, block, s2.at[at, d - 1, h, e - 1], r2.at[at, d - 1, h, e - 1], peer)

    def third(d, h):
        j = (p.inner - d + 4) % 4
        block = gathered.at[j, halves[h]]
        return remote(block, block, s3.at[at, d - 1, h], r3.at[at, d - 1, h], p.sibling())

    order = (1, 3, 2)
    every = [(d, h) for d in order for h in range(2)]

    def go1():
        for d, h in every:
            first(d, h).start()

    def go2(d):
        for h in range(2):
            first(d, h).wait_recv()
            for e in (1, 3, 2):
                second(d, h, e).start()

    def go3(d):
        for h in range(2):
            for e in (1, 3, 2):
                second(d, h, e).wait_recv()
            third(d, h).start()

    def end():
        for d, h in every:
            third(d, h).wait_recv()
        for d, h in every:
            first(d, h).wait_send()
            third(d, h).wait_send()
            for e in (1, 3, 2):
                second(d, h, e).wait_send()

    return order, go1, go2, go3, end


def spread_sems(n):
    return [DMA((n, 3, 2)), DMA((n, 3, 2)), DMA((n, 3, 2, 3)), DMA((n, 3, 2, 3)), DMA((n, 3, 2)), DMA((n, 3, 2))]


def square_peers(p):
    return (
        [p.along_z(d) for d in (1, 2, 3)]
        + [p.along_y(d) for d in (1, 2, 3)]
        + [p.along_x(d) for d in (1, 2, 3)]
        + [p.sibling()]
    )


def att_in_kernel(w, r, gw, gr, s1, r1, s2, r2, s3, r3, sr, rr, local):
    p = Place()
    copies = [
        pltpu.make_async_copy(w, gw.at[p.inner], local.at[0]),
        pltpu.make_async_copy(r, gr.at[p.inner], local.at[1]),
    ]
    for copy in copies:
        copy.start()
    meet(square_peers(p))
    order, go1, go2, go3, end = spread_over_z(0, w, gw, 1024, p, (s1, r1, s2, r2, s3, r3))
    go1()
    routers = [remote(r, gr.at[p.inner], sr.at[d - 1], rr.at[d - 1], p.along_z(d)) for d in (1, 2, 3)]
    for copy in routers:
        copy.start()
    for d in order:
        go2(d)
    for d in order:
        go3(d)
    end()
    for copy in routers:
        copy.wait()
    for copy in copies:
        copy.wait()


def gather_att_in(att_in, router_t):
    return pl.pallas_call(
        att_in_kernel,
        out_shape=(
            jax.ShapeDtypeStruct((4, 1024, 768), BF),
            jax.ShapeDtypeStruct((4, 8, 1024), BF),
        ),
        in_specs=[ANY, ANY],
        out_specs=(ANY, ANY),
        scratch_shapes=spread_sems(1) + [DMA((3,)), DMA((3,)), DMA((2,))],
        compiler_params=pltpu.CompilerParams(collective_id=1, has_side_effects=True, vmem_limit_bytes=2**20),
        name="gather_att_in",
    )(att_in, router_t)


def kv_kernel(kv, w, gk, gw, s1, r1, s2, r2, s3, r3, sz, rz, sx, rx, sc, rc, local):
    p = Place()
    copies = [
        pltpu.make_async_copy(w, gw.at[p.inner], local.at[0]),
        pltpu.make_async_copy(kv, gk.at[p.outer, p.inner], local.at[1]),
    ]
    for copy in copies:
        copy.start()
    meet(square_peers(p))
    order, go1, go2, go3, end = spread_over_z(0, w, gw, 512, p, (s1, r1, s2, r2, s3, r3))
    zs = [remote(kv, gk.at[p.outer, p.inner], sz.at[d - 1], rz.at[d - 1], p.along_z(d)) for d in (1, 2, 3)]
    xs = [
        remote(gk.at[p.outer], gk.at[p.outer], sx.at[d - 1], rx.at[d - 1], p.along_x(d)) for d in (1, 2, 3)
    ]
    cs = []
    for d in range(4):
        o = ((p.x - d + 4) % 4) * 2 + p.c
        cs.append(remote(gk.at[o], gk.at[o], sc.at[d], rc.at[d], p.sibling()))
    for copy in zs:
        copy.start()
    go1()
    copies[1].wait()
    for copy in zs:
        copy.wait_recv()
    for copy in (xs[0], xs[2], xs[1]):
        copy.start()
    cs[0].start()
    for d in order:
        go2(d)
    for d in (1, 3, 2):
        xs[d - 1].wait_recv()
        cs[d].start()
    for d in order:
        go3(d)
    end()
    for copy in cs:
        copy.wait()
    for copy in zs + xs:
        copy.wait_send()
    copies[0].wait()


def gather_kv(kv, att_out):
    return pl.pallas_call(
        kv_kernel,
        out_shape=(
            jax.ShapeDtypeStruct((8, 4, ROWS, 256), BF),
            jax.ShapeDtypeStruct((4, 512, 1024), BF),
        ),
        in_specs=[ANY, ANY],
        out_specs=(ANY, ANY),
        scratch_shapes=spread_sems(1)
        + [DMA((3,)), DMA((3,)), DMA((3,)), DMA((3,)), DMA((4,)), DMA((4,)), DMA((2,))],
        compiler_params=pltpu.CompilerParams(collective_id=2, has_side_effects=True, vmem_limit_bytes=2**20),
        name="gather_kv",
    )(kv, att_out)


class Weights:
    def __init__(self, p, own, gathered, sems):
        self.p, self.own, self.gathered = p, own, gathered
        self.ns, self.fr, self.ps, self.sr, self.ys, self.yr = sems
        self.k = p.y % 2
        self.step = 2 * p.zl - 1

    def part(self, ref, kind, e, c):
        span = pl.ds(pl.multiple_of(c * 512, 512), 512)
        return ref.at[e, span, :] if kind == 0 else ref.at[e, :, span]

    def chunk(self, kind, shard, c):
        return self.part(self.gathered[kind], kind, ((shard + 8) % 4) * 2 + self.k, c)

    def to_next(self, kind, m, t):
        p = self.p
        if t < 2:
            src = self.part(self.own[kind], kind, self.k, 2 * m + t)
            dst = self.chunk(kind, p.inner, 2 * m + t)
        else:
            src = dst = self.chunk(kind, p.inner - self.step, 2 * m + 1 - p.zl)
        return remote(src, dst, self.ns.at[kind, m, t], self.fr.at[kind, m, t], p.beyond())

    def far(self, kind, m, t):
        p = self.p
        return (p.inner + self.step, 2 * m + t) if t < 2 else (p.inner + 2, 2 * m + p.zl)

    def near(self, kind, m, t):
        p = self.p
        return (p.inner - self.step, 2 * m + t) if t < 2 else (p.inner + 2, 2 * m + 1 - p.zl)

    def forward(self, kind, m, t):
        block = self.chunk(kind, *self.far(kind, m, t))
        return remote(block, block, self.ps.at[kind, m, t], self.sr.at[kind, m, t], self.p.pair())

    def sideways(self, kind, m, t, which):
        shard, c = (self.far, self.near)[which](kind, m, t)
        block = self.chunk(kind, shard, c)
        peer = self.p.along_y(5 - 2 * (c % 2))
        return remote(block, block, self.ys.at[kind, m, t, which], self.yr.at[kind, m, t, which], peer)

    def begin(self, kind, m):
        for t in range(2):
            self.to_next(kind, m, t).start()

    def turn(self, kind, m, after=None):
        if after is not None:
            self.begin(*after)
        for t in range(3):
            self.to_next(kind, m, t).wait_recv()
            self.forward(kind, m, t).start()
            self.sideways(kind, m, t, 0).start()
            self.forward(kind, m, t).wait_recv()
            self.sideways(kind, m, t, 1).start()
            if t == 1:
                self.to_next(kind, m, 2).start()

    def settle(self, kind, m):
        for t in range(3):
            for which in range(2):
                self.sideways(kind, m, t, which).wait_recv()

    def drain(self, kind, m):
        for t in range(3):
            self.to_next(kind, m, t).wait_send()
            self.forward(kind, m, t).wait_send()
            for which in range(2):
                self.sideways(kind, m, t, which).wait_send()

    def peers(self):
        p = self.p
        return [p.beyond(), p.pair(), p.along_y(1), p.along_y(3)]


def weight_sems():
    return [DMA((2, 4, 3))] * 4 + [DMA((2, 4, 3, 2))] * 2


def moe_kernel(
    ext, hs, up, down, out, gup, gdn,
    xall, acc, hid, wbuf, dbuf, part, pairbuf, xbuf,
    ns, fr, ps, sr, ys, yr, ts, tr, us, ur, vs, vr, es, er, qs, qr, local, load,
):
    p = Place()
    w = Weights(p, (up, down), (gup, gdn), (ns, fr, ps, sr, ys, yr))
    own_copies = [
        pltpu.make_async_copy(up, gup.at[pl.ds(2 * p.inner, 2)], local.at[0]),
        pltpu.make_async_copy(down, gdn.at[pl.ds(2 * p.inner, 2)], local.at[1]),
    ]
    for copy in own_copies:
        copy.start()
    meet(w.peers() + [p.along_x(1), p.along_x(2), p.along_x(3), p.sibling()])
    w.begin(0, 0)

    def rows(o, h):
        return xall.at[o, pl.ds(64 * h, 64), :]

    def block(d):
        return ((p.x + d) % 4) * 2 + p.c

    def mine(d, h):
        src = ext.at[pl.ds(64 * h, 64), :]
        return remote(src, rows(p.outer, h), ts.at[(d - 1) // 2, h], tr.at[(d - 1) // 2, h], p.along_x(d))

    def relay(d):
        h = (d - 1) // 2
        src = rows(block(4 - d), h)
        return remote(src, src, us.at[h], ur.at[h], p.along_x(d))

    def across(d, h):
        src = ext.at[pl.ds(64 * h, 64), :] if d == 0 else rows(block(d), h)
        return remote(src, rows(block(d), h), vs.at[d, h], vr.at[d, h], p.sibling())

    for h in range(2):
        for d in (1, 3):
            mine(d, h if d == 1 else 1 - h).start()
    for h in range(2):
        across(0, h).start()
    keep = pltpu.make_async_copy(ext, xall.at[p.outer], local.at[2])
    keep.start()

    w.turn(0, 0, (0, 1))
    mine(1, 0).wait_recv()
    relay(1).start()
    across(3, 0).start()
    mine(3, 1).wait_recv()
    relay(3).start()
    across(1, 1).start()
    mine(1, 1).wait_recv()
    across(3, 1).start()
    mine(3, 0).wait_recv()
    across(1, 0).start()
    w.turn(0, 1, (0, 2))
    for d in (1, 3):
        relay(d).wait_recv()
        across(2, (d - 1) // 2).start()
    for copy in own_copies:
        copy.wait()

    def load_up(m):
        return pltpu.make_async_copy(
            gup.at[:, pl.ds(1024 * m, 1024), :], wbuf.at[m % 2], load.at[m % 2]
        )

    def load_down(m):
        return pltpu.make_async_copy(
            gdn.at[:, :, pl.ds(1024 * m, 1024)], dbuf.at[m % 2], load.at[m % 2]
        )

    def run_up(m):
        xs = xall.at[:, :, pl.ds(1024 * m, 1024)]

        def one(e, carry):
            got = jnp.dot(
                xs[...].reshape(1024, 1024), wbuf[m % 2, e], preferred_element_type=F32
            )
            if m == 0:
                acc[e] = got
            else:
                acc[e] += got
            return carry

        lax.fori_loop(0, 8, one, 0)

    def gate():
        names = lax.broadcasted_iota(jnp.int32, (128, 256), 0) % 64
        shares = xall[:, :, D:].reshape(1024, 128)

        def one(e, carry):
            pick = jnp.where(names == p.outer * 8 + e, 1.0, 0.0).astype(BF)
            scale = jnp.dot(shares, pick, preferred_element_type=F32)
            hid[:, pl.ds(pl.multiple_of(256 * e, 256), 256)] = (jnp.maximum(acc[e], 0.0) * scale).astype(BF)
            return carry

        lax.fori_loop(0, 8, one, 0)

    def run_down(m):
        def one(n, carry):
            span = pl.ds(pl.multiple_of(256 * n, 256), 256)
            weights = dbuf[m % 2, :, :, span].reshape(2048, 256)
            got = jnp.dot(hid[...], weights, preferred_element_type=F32)
            part[m, :, :, :, span] = got.astype(BF).reshape(4, 2, 128, 256)
            return carry

        lax.fori_loop(0, 4, one, 0)

    def swap(m):
        return remote(part.at[m, :, 1 - p.c], pairbuf.at[m], es.at[m], er.at[m], p.sibling())

    def give(m, d):
        there = (p.x + d) % 4
        return remote(part.at[m, there, p.c], xbuf.at[m, d - 1], qs.at[m, d - 1], qr.at[m, d - 1], p.along_x(d))

    def add_pair(m):
        swap(m).wait_recv()
        for d in (1, 3, 2):
            there = (p.x + d) % 4
            total = part[m, there, p.c].astype(F32) + pairbuf[m, there].astype(F32)
            part[m, there, p.c] = total.astype(BF)
            give(m, d).start()

    def finish(m):
        span = pl.ds(1024 * m, 1024)
        total = hs[:, span] + part[m, p.x, p.c].astype(F32) + pairbuf[m, p.x].astype(F32)
        for d in (1, 3, 2):
            give(m, d).wait_recv()
            total += xbuf[m, d - 1].astype(F32)
        out[:, span] = total.astype(BF)

    w.settle(0, 0)
    load_up(0).start()
    w.turn(0, 2, (0, 3))
    keep.wait()
    for d in range(4):
        for h in range(2):
            across(d, h).wait_recv()
    w.settle(0, 1)
    load_up(1).start()
    load_up(0).wait()
    run_up(0)
    w.turn(0, 3, (1, 0))
    w.settle(0, 2)
    load_up(2).start()
    load_up(1).wait()
    run_up(1)
    w.turn(1, 0, (1, 1))
    w.settle(0, 3)
    load_up(3).start()
    load_up(2).wait()
    run_up(2)
    w.settle(1, 0)
    load_down(0).start()
    load_up(3).wait()
    run_up(3)
    gate()
    w.turn(1, 1, (1, 2))
    w.settle(1, 1)
    load_down(1).start()
    load_down(0).wait()
    run_down(0)
    swap(0).start()
    w.turn(1, 2, (1, 3))
    w.settle(1, 2)
    load_down(2).start()
    load_down(1).wait()
    run_down(1)
    swap(1).start()
    add_pair(0)
    w.turn(1, 3)
    load_down(2).wait()
    run_down(2)
    swap(2).start()
    add_pair(1)
    finish(0)
    w.settle(1, 3)
    load_down(3).start()
    load_down(3).wait()
    run_down(3)
    swap(3).start()
    add_pair(2)
    add_pair(3)
    for m in (1, 2, 3):
        finish(m)
    for kind in range(2):
        for m in range(4):
            w.drain(kind, m)
    for h in range(2):
        for d in (1, 3):
            mine(d, h).wait_send()
        for d in range(4):
            across(d, h).wait_send()
    for d in (1, 3):
        relay(d).wait_send()
    for m in range(4):
        swap(m).wait_send()
        for d in (1, 2, 3):
            give(m, d).wait_send()


def moe(ext, hidden_state, w_up, w_down):
    return pl.pallas_call(
        moe_kernel,
        out_shape=(
            jax.ShapeDtypeStruct((ROWS, D), BF),
            jax.ShapeDtypeStruct((8, D, 256), BF),
            jax.ShapeDtypeStruct((8, 256, D), BF),
        ),
        in_specs=[VM, VM, ANY, ANY],
        out_specs=(VM, ANY, ANY),
        scratch_shapes=[
            pltpu.VMEM((8, ROWS, EXT), BF),
            pltpu.VMEM((8, 1024, 256), F32),
            pltpu.VMEM((1024, 2048), BF),
            pltpu.VMEM((2, 8, 1024, 256), BF),
            pltpu.VMEM((2, 8, 256, 1024), BF),
            pltpu.VMEM((4, 4, 2, ROWS, 1024), BF),
            pltpu.VMEM((4, 4, ROWS, 1024), BF),
            pltpu.VMEM((4, 3, ROWS, 1024), BF),
        ]
        + weight_sems()
        + [
            DMA((2, 2)), DMA((2, 2)), DMA((2,)), DMA((2,)), DMA((4, 2)), DMA((4, 2)),
            DMA((4,)), DMA((4,)), DMA((4, 3)), DMA((4, 3)), DMA((3,)), DMA((2,)),
        ],
        compiler_params=pltpu.CompilerParams(collective_id=3, has_side_effects=True, vmem_limit_bytes=60 * 2**20),
        name="experts",
    )(ext, hidden_state, w_up, w_down)[0]


def on_device(
    tokens,
    att_ids,
    mlp_ids,
    att_gain,
    att_in,
    att_router,
    att_out,
    mlp_gain,
    mlp_router,
    w_up,
    w_down,
):
    row_count = tokens.shape[0]
    head_width = HEADS * HDIM
    in_all, router_all = gather_att_in(att_in, att_router.T)
    normed = rms_norm(tokens, att_gain).astype(BF)
    proj = jnp.dot(normed, in_all.reshape(D, 768), preferred_element_type=F32)
    att_logit = jnp.einsum(
        "tsk,snk->tn", normed.reshape(row_count, 4, 1024), router_all, preferred_element_type=F32
    )
    query = proj[:, :head_width].astype(BF).reshape(row_count, HEADS, HDIM)
    keys = proj[:, head_width : 2 * head_width].astype(BF)
    value_all = proj[:, 2 * head_width :].reshape(row_count, HEADS, ATT_EXP, HDIM)
    chosen = jnp.sum(
        (att_ids[..., None] == jnp.arange(ATT_EXP)[None, None, None, :]).astype(F32), axis=2
    )
    att_weight = jax.nn.sigmoid(att_logit.reshape(row_count, HEADS, ATT_EXP)) * chosen
    values = jnp.sum(att_weight[..., None] * value_all, axis=2).astype(BF).reshape(row_count, head_width)
    kv_all, out_all = gather_kv(jnp.concatenate([keys, values], axis=1), att_out)
    kv_rows = kv_all.reshape(-1, 4, HDIM)
    first_row = lax.axis_index(("outer", "inner")) * row_count
    query_position = first_row + jnp.arange(row_count)
    scores = jnp.einsum("thd,shd->hts", query, kv_rows[:, :HEADS], preferred_element_type=F32) * HDIM ** (-0.5)
    visible = jnp.arange(kv_rows.shape[0])[None, None, :] <= query_position[None, :, None]
    scores = jnp.where(visible, scores, -1e30)
    weights = jnp.exp(scores - jnp.max(scores, axis=-1, keepdims=True))
    total = jnp.sum(weights, axis=-1)
    attended = jnp.einsum("hts,shd->thd", weights.astype(BF), kv_rows[:, HEADS:], preferred_element_type=F32)
    attended = attended / total.T[..., None]
    head_normed = attended * lax.rsqrt(jnp.mean(attended * attended, axis=-1, keepdims=True) + epsilon)
    mixed = (head_normed[:, :, None, :] * att_weight[..., None]).reshape(row_count, HEADS * ATT_EXP * HDIM)
    mixed = mixed.astype(BF)
    att_result = jnp.einsum("tk,skn->tsn", mixed, out_all, preferred_element_type=F32).reshape(row_count, D)
    hidden_state = tokens.astype(F32) + att_result
    mlp_in = rms_norm(hidden_state, mlp_gain).astype(BF)
    logits = jnp.dot(mlp_in, mlp_router, preferred_element_type=F32)
    picked = jnp.any(mlp_ids[..., None] == jnp.arange(mlp_router.shape[1])[None, None, :], axis=1)
    gates = jnp.where(picked, jax.nn.sigmoid(logits), 0.0)
    high = lax.reduce_precision(gates, 8, 7)
    ext = jnp.concatenate([mlp_in, high.astype(BF), (gates - high).astype(BF)], axis=1)
    return moe(ext, hidden_state, w_up, w_down)


def solution(mesh):
    in_specs = (
        P(("seq", "outer", "inner"), None),
        P(("seq", "outer", "inner"), None, None),
        P(("seq", "outer", "inner"), None),
        P(),
        P("inner", None),
        P("inner", None),
        P(None, "inner"),
        P(),
        P(),
        P(("outer", "inner"), None, None),
        P(("outer", "inner"), None, None),
    )
    out_specs = P(("seq", "outer", "inner"), None)
    return jax.shard_map(
        on_device, mesh=mesh, in_specs=in_specs, out_specs=out_specs, check_vma=False
    )
```

```python
import functools

import jax
import jax.numpy as jnp
from jax import lax
from jax.experimental import pallas as pl
from jax.experimental.pallas import tpu as pltpu
from jax.sharding import PartitionSpec as P

D = 4096
HEADS = 2
HDIM = 64
ATT_EXP = 4
EXT = D + 128
ROWS = 128
epsilon = 1e-05
MESH = pl.DeviceIdType.MESH
ANY = pl.BlockSpec(memory_space=pl.ANY)
VM = pl.BlockSpec(memory_space=pltpu.VMEM)
DMA = pltpu.SemaphoreType.DMA
BF = jnp.bfloat16
F32 = jnp.float32


def rms_norm(values_in, gain_vector):
    floats = values_in.astype(F32)
    return (
        floats
        * lax.rsqrt(jnp.mean(floats * floats, axis=-1, keepdims=True) + epsilon)
        * gain_vector
    )


class Place:
    def __init__(self):
        self.seq, self.outer, self.inner = (lax.axis_index(a) for a in ("seq", "outer", "inner"))
        self.zl, self.y = self.seq // 4, self.seq % 4
        self.x, self.c = self.outer // 2, self.outer % 2

    def along_z(self, d):
        return (self.seq, self.outer, (self.inner + d) % 4)

    def along_y(self, d):
        return (self.zl * 4 + (self.y + d) % 4, self.outer, self.inner)

    def along_x(self, d):
        return (self.seq, ((self.x + d) % 4) * 2 + self.c, self.inner)

    def sibling(self):
        return (self.seq, self.x * 2 + 1 - self.c, self.inner)

    def pair(self):
        return ((1 - self.zl) * 4 + self.y, self.outer, self.inner)

    def beyond(self):
        return ((1 - self.zl) * 4 + self.y, self.outer, (self.inner + 2 * self.zl - 1) % 4)


def meet(peers):
    barrier = pltpu.get_barrier_semaphore()
    for peer in peers:
        pl.semaphore_signal(barrier, inc=1, device_id=peer, device_id_type=MESH)
    pl.semaphore_wait(barrier, len(peers))


def remote(src, dst, send, recv, peer):
    return pltpu.make_async_remote_copy(
        src_ref=src, dst_ref=dst, send_sem=send, recv_sem=recv, device_id=peer, device_id_type=MESH
    )


def spread_over_z(at, own, gathered, full, p, sems):
    s1, r1, s2, r2, s3, r3 = sems
    n = full // 16
    spans = (
        pl.ds(pl.multiple_of(p.c * (4 * n) + p.y * n, n), n),
        pl.ds(pl.multiple_of(8 * n + p.c * (4 * n) + p.x * n, n), n),
    )
    halves = tuple(pl.ds(pl.multiple_of(8 * n * h + p.c * (4 * n), 4 * n), 4 * n) for h in range(2))

    def first(d, h):
        return remote(
            own.at[spans[h]], gathered.at[p.inner, spans[h]], s1.at[at, d - 1, h], r1.at[at, d - 1, h], p.along_z(d)
        )

    def second(d, h, e):
        j = (p.inner - d + 4) % 4
        peer = p.along_y(e) if h == 0 else p.along_x(e)
        block = gathered.at[j, spans[h]]
        return remote(block, block, s2.at[at, d - 1, h, e - 1], r2.at[at, d - 1, h, e - 1], peer)

    def third(d, h):
        j = (p.inner - d + 4) % 4
        block = gathered.at[j, halves[h]]
        return remote(block, block, s3.at[at, d - 1, h], r3.at[at, d - 1, h], p.sibling())

    order = (1, 3, 2)
    every = [(d, h) for d in order for h in range(2)]

    def go1():
        for d, h in every:
            first(d, h).start()

    def go2(d):
        for h in range(2):
            first(d, h).wait_recv()
            for e in (1, 3, 2):
                second(d, h, e).start()

    def go3(d):
        for h in range(2):
            for e in (1, 3, 2):
                second(d, h, e).wait_recv()
            third(d, h).start()

    def end():
        for d, h in every:
            third(d, h).wait_recv()
        for d, h in every:
            first(d, h).wait_send()
            third(d, h).wait_send()
            for e in (1, 3, 2):
                second(d, h, e).wait_send()

    return order, go1, go2, go3, end


def spread_sems(n):
    return [DMA((n, 3, 2)), DMA((n, 3, 2)), DMA((n, 3, 2, 3)), DMA((n, 3, 2, 3)), DMA((n, 3, 2)), DMA((n, 3, 2))]


def square_peers(p):
    return (
        [p.along_z(d) for d in (1, 2, 3)]
        + [p.along_y(d) for d in (1, 2, 3)]
        + [p.along_x(d) for d in (1, 2, 3)]
        + [p.sibling()]
    )


def att_in_kernel(w, r, gw, gr, s1, r1, s2, r2, s3, r3, sr, rr, local):
    p = Place()
    copies = [
        pltpu.make_async_copy(w, gw.at[p.inner], local.at[0]),
        pltpu.make_async_copy(r, gr.at[p.inner], local.at[1]),
    ]
    for copy in copies:
        copy.start()
    meet(square_peers(p))
    order, go1, go2, go3, end = spread_over_z(0, w, gw, 1024, p, (s1, r1, s2, r2, s3, r3))
    go1()
    routers = [remote(r, gr.at[p.inner], sr.at[d - 1], rr.at[d - 1], p.along_z(d)) for d in (1, 2, 3)]
    for copy in routers:
        copy.start()
    for d in order:
        go2(d)
    for d in order:
        go3(d)
    end()
    for copy in routers:
        copy.wait()
    for copy in copies:
        copy.wait()


def gather_att_in(att_in, router_t):
    return pl.pallas_call(
        att_in_kernel,
        out_shape=(
            jax.ShapeDtypeStruct((4, 1024, 768), BF),
            jax.ShapeDtypeStruct((4, 8, 1024), BF),
        ),
        in_specs=[ANY, ANY],
        out_specs=(ANY, ANY),
        scratch_shapes=spread_sems(1) + [DMA((3,)), DMA((3,)), DMA((2,))],
        compiler_params=pltpu.CompilerParams(collective_id=1, has_side_effects=True, vmem_limit_bytes=2**20),
        name="gather_att_in",
    )(att_in, router_t)


def kv_kernel(kv, w, gk, gw, s1, r1, s2, r2, s3, r3, sz, rz, sx, rx, sc, rc, local):
    p = Place()
    copies = [
        pltpu.make_async_copy(w, gw.at[p.inner], local.at[0]),
        pltpu.make_async_copy(kv, gk.at[p.outer, p.inner], local.at[1]),
    ]
    for copy in copies:
        copy.start()
    meet(square_peers(p))
    order, go1, go2, go3, end = spread_over_z(0, w, gw, 512, p, (s1, r1, s2, r2, s3, r3))
    zs = [remote(kv, gk.at[p.outer, p.inner], sz.at[d - 1], rz.at[d - 1], p.along_z(d)) for d in (1, 2, 3)]
    xs = [
        remote(gk.at[p.outer], gk.at[p.outer], sx.at[d - 1], rx.at[d - 1], p.along_x(d)) for d in (1, 2, 3)
    ]
    cs = []
    for d in range(4):
        o = ((p.x - d + 4) % 4) * 2 + p.c
        cs.append(remote(gk.at[o], gk.at[o], sc.at[d], rc.at[d], p.sibling()))
    for copy in zs:
        copy.start()
    go1()
    copies[1].wait()
    for copy in zs:
        copy.wait_recv()
    for copy in (xs[0], xs[2], xs[1]):
        copy.start()
    cs[0].start()
    for d in order:
        go2(d)
    for d in (1, 3, 2):
        xs[d - 1].wait_recv()
        cs[d].start()
    for d in order:
        go3(d)
    end()
    for copy in cs:
        copy.wait()
    for copy in zs + xs:
        copy.wait_send()
    copies[0].wait()


def gather_kv(kv, att_out):
    return pl.pallas_call(
        kv_kernel,
        out_shape=(
            jax.ShapeDtypeStruct((8, 4, ROWS, 256), BF),
            jax.ShapeDtypeStruct((4, 512, 1024), BF),
        ),
        in_specs=[ANY, ANY],
        out_specs=(ANY, ANY),
        scratch_shapes=spread_sems(1)
        + [DMA((3,)), DMA((3,)), DMA((3,)), DMA((3,)), DMA((4,)), DMA((4,)), DMA((2,))],
        compiler_params=pltpu.CompilerParams(collective_id=2, has_side_effects=True, vmem_limit_bytes=2**20),
        name="gather_kv",
    )(kv, att_out)


class Weights:
    def __init__(self, p, own, gathered, sems):
        self.p, self.own, self.gathered = p, own, gathered
        self.ns, self.fr, self.ps, self.sr, self.ys, self.yr = sems
        self.k = p.y % 2
        self.step = 2 * p.zl - 1

    def part(self, ref, kind, e, c):
        span = pl.ds(pl.multiple_of(c * 512, 512), 512)
        return ref.at[e, span, :] if kind == 0 else ref.at[e, :, span]

    def chunk(self, kind, shard, c):
        return self.part(self.gathered[kind], kind, ((shard + 8) % 4) * 2 + self.k, c)

    def to_next(self, kind, m, t):
        p = self.p
        if t < 2:
            src = self.part(self.own[kind], kind, self.k, 2 * m + t)
            dst = self.chunk(kind, p.inner, 2 * m + t)
        else:
            src = dst = self.chunk(kind, p.inner - self.step, 2 * m + 1 - p.zl)
        return remote(src, dst, self.ns.at[kind, m, t], self.fr.at[kind, m, t], p.beyond())

    def far(self, kind, m, t):
        p = self.p
        return (p.inner + self.step, 2 * m + t) if t < 2 else (p.inner + 2, 2 * m + p.zl)

    def near(self, kind, m, t):
        p = self.p
        return (p.inner - self.step, 2 * m + t) if t < 2 else (p.inner + 2, 2 * m + 1 - p.zl)

    def forward(self, kind, m, t):
        block = self.chunk(kind, *self.far(kind, m, t))
        return remote(block, block, self.ps.at[kind, m, t], self.sr.at[kind, m, t], self.p.pair())

    def sideways(self, kind, m, t, which):
        shard, c = (self.far, self.near)[which](kind, m, t)
        block = self.chunk(kind, shard, c)
        peer = self.p.along_y(5 - 2 * (c % 2))
        return remote(block, block, self.ys.at[kind, m, t, which], self.yr.at[kind, m, t, which], peer)

    def begin(self, kind, m):
        for t in range(2):
            self.to_next(kind, m, t).start()

    def take_far(self, kind, m, t):
        self.to_next(kind, m, t).wait_recv()
        self.forward(kind, m, t).start()
        self.sideways(kind, m, t, 0).start()

    def take_near(self, kind, m, t):
        self.forward(kind, m, t).wait_recv()
        self.sideways(kind, m, t, 1).start()

    def turn(self, q, last, between=None):
        kind, m = q // 4, q % 4
        before = ((q - 1) // 4, (q - 1) % 4)
        if q < last:
            self.begin((q + 1) // 4, (q + 1) % 4)
        if q <= last:
            self.take_far(kind, m, 0)
            self.take_far(kind, m, 1)
        if q > 0:
            self.take_far(*before, 2)
        if between is not None:
            between()
        if q <= last:
            self.take_near(kind, m, 0)
            self.take_near(kind, m, 1)
            self.to_next(kind, m, 2).start()
        if q > 0:
            self.take_near(*before, 2)

    def settle(self, kind, m):
        for t in range(3):
            for which in range(2):
                self.sideways(kind, m, t, which).wait_recv()

    def drain(self, kind, m):
        for t in range(3):
            self.to_next(kind, m, t).wait_send()
            self.forward(kind, m, t).wait_send()
            for which in range(2):
                self.sideways(kind, m, t, which).wait_send()

    def peers(self):
        p = self.p
        return [p.beyond(), p.pair(), p.along_y(1), p.along_y(3)]


def weight_sems():
    return [DMA((2, 4, 3))] * 4 + [DMA((2, 4, 3, 2))] * 2


def moe_kernel(
    ext, hs, up, down, out, gup, gdn,
    xall, acc, hid, wbuf, dbuf, part, pairbuf, xbuf,
    ns, fr, ps, sr, ys, yr, ts, tr, us, ur, vs, vr, es, er, qs, qr, local, load,
):
    p = Place()
    w = Weights(p, (up, down), (gup, gdn), (ns, fr, ps, sr, ys, yr))
    meet(w.peers() + [p.along_x(1), p.along_x(2), p.along_x(3), p.sibling()])
    w.begin(0, 0)

    def rows(o, h):
        return xall.at[o, pl.ds(64 * h, 64), :]

    def block(d):
        return ((p.x + d) % 4) * 2 + p.c

    def mine(d, h):
        src = ext.at[pl.ds(64 * h, 64), :]
        return remote(src, rows(p.outer, h), ts.at[(d - 1) // 2, h], tr.at[(d - 1) // 2, h], p.along_x(d))

    def relay(d):
        h = (d - 1) // 2
        src = rows(block(4 - d), h)
        return remote(src, src, us.at[h], ur.at[h], p.along_x(d))

    def across(d, h):
        src = ext.at[pl.ds(64 * h, 64), :] if d == 0 else rows(block(d), h)
        return remote(src, rows(block(d), h), vs.at[d, h], vr.at[d, h], p.sibling())

    for h in range(2):
        for d in (1, 3):
            mine(d, h if d == 1 else 1 - h).start()
    for h in range(2):
        across(0, h).start()
    keep = pltpu.make_async_copy(ext, xall.at[p.outer], local.at[2])
    keep.start()

    def loads(m, own, gathered, buffer, view):
        for d in range(4):
            two = pl.ds(2 * ((p.inner + d) % 4), 2)
            src = view(own, slice(None)) if d == 0 else view(gathered, two)
            yield pltpu.make_async_copy(src, buffer.at[m % 2, two], load.at[m % 2, d])

    def load_up(m):
        return loads(m, up, gup, wbuf, lambda ref, two: ref.at[two, pl.ds(1024 * m, 1024), :])

    def load_down(m):
        return loads(m, down, gdn, dbuf, lambda ref, two: ref.at[two, :, pl.ds(1024 * m, 1024)])

    def fetch(q):
        w.settle(q // 4, q % 4)
        for copy in (load_up, load_down)[q // 4](q % 4):
            copy.start()

    def use(q):
        for copy in (load_up, load_down)[q // 4](q % 4):
            copy.wait()
        if q < 4:
            run_up(q)
        else:
            run_down(q - 4)
            swap(q - 4).start()

    def run_up(m):
        xs = xall.at[:, :, pl.ds(1024 * m, 1024)]

        def one(e, carry):
            got = jnp.dot(
                xs[...].reshape(1024, 1024), wbuf[m % 2, e], preferred_element_type=F32
            )
            if m == 0:
                acc[e] = got
            else:
                acc[e] += got
            return carry

        lax.fori_loop(0, 8, one, 0)

    def gate():
        names = lax.broadcasted_iota(jnp.int32, (128, 256), 0) % 64
        shares = xall[:, :, D:].reshape(1024, 128)

        def one(e, carry):
            pick = jnp.where(names == p.outer * 8 + e, 1.0, 0.0).astype(BF)
            scale = jnp.dot(shares, pick, preferred_element_type=F32)
            hid[:, pl.ds(pl.multiple_of(256 * e, 256), 256)] = (jnp.maximum(acc[e], 0.0) * scale).astype(BF)
            return carry

        lax.fori_loop(0, 8, one, 0)

    def run_down(m):
        def one(n, carry):
            span = pl.ds(pl.multiple_of(256 * n, 256), 256)
            weights = dbuf[m % 2, :, :, span].reshape(2048, 256)
            got = jnp.dot(hid[...], weights, preferred_element_type=F32)
            part[m, :, :, :, span] = got.astype(BF).reshape(4, 2, 128, 256)
            return carry

        lax.fori_loop(0, 4, one, 0)

    def swap(m):
        return remote(part.at[m, :, 1 - p.c], pairbuf.at[m], es.at[m], er.at[m], p.sibling())

    def give(m, d):
        there = (p.x + d) % 4
        return remote(part.at[m, there, p.c], xbuf.at[m, d - 1], qs.at[m, d - 1], qr.at[m, d - 1], p.along_x(d))

    def add_pair(m):
        swap(m).wait_recv()
        for d in (1, 3, 2):
            there = (p.x + d) % 4
            total = part[m, there, p.c].astype(F32) + pairbuf[m, there].astype(F32)
            part[m, there, p.c] = total.astype(BF)
            give(m, d).start()

    def finish(m):
        span = pl.ds(1024 * m, 1024)
        total = hs[:, span] + part[m, p.x, p.c].astype(F32) + pairbuf[m, p.x].astype(F32)
        for d in (1, 3, 2):
            give(m, d).wait_recv()
            total += xbuf[m, d - 1].astype(F32)
        out[:, span] = total.astype(BF)

    def tokens_1():
        mine(1, 0).wait_recv()
        relay(1).start()
        mine(3, 1).wait_recv()
        relay(3).start()
        across(3, 0).start()
        across(1, 1).start()

    def tokens_2():
        mine(1, 1).wait_recv()
        across(3, 1).start()
        mine(3, 0).wait_recv()
        across(1, 0).start()
        for d in (1, 3):
            relay(d).wait_recv()
            across(2, (d - 1) // 2).start()
        fetch(0)

    def first_use():
        keep.wait()
        for d in range(4):
            for h in range(2):
                across(d, h).wait_recv()
        use(0)
        fetch(1)

    def step_4():
        use(1)
        fetch(2)

    def step_5():
        use(2)
        fetch(3)

    def step_6():
        use(3)
        gate()
        fetch(4)

    def step_7():
        use(4)
        fetch(5)

    def step_8():
        add_pair(0)
        use(5)
        fetch(6)

    steps = (None, tokens_1, tokens_2, first_use, step_4, step_5, step_6, step_7, step_8)
    for q in range(9):
        w.turn(q, 7, steps[q])
    add_pair(1)
    use(6)
    fetch(7)
    finish(0)
    add_pair(2)
    use(7)
    finish(1)
    add_pair(3)
    finish(2)
    finish(3)
    for kind in range(2):
        for m in range(4):
            w.drain(kind, m)
    for h in range(2):
        for d in (1, 3):
            mine(d, h).wait_send()
        for d in range(4):
            across(d, h).wait_send()
    for d in (1, 3):
        relay(d).wait_send()
    for m in range(4):
        swap(m).wait_send()
        for d in (1, 2, 3):
            give(m, d).wait_send()


def moe(ext, hidden_state, w_up, w_down):
    return pl.pallas_call(
        moe_kernel,
        out_shape=(
            jax.ShapeDtypeStruct((ROWS, D), BF),
            jax.ShapeDtypeStruct((8, D, 256), BF),
            jax.ShapeDtypeStruct((8, 256, D), BF),
        ),
        in_specs=[VM, VM, ANY, ANY],
        out_specs=(VM, ANY, ANY),
        scratch_shapes=[
            pltpu.VMEM((8, ROWS, EXT), BF),
            pltpu.VMEM((8, 1024, 256), F32),
            pltpu.VMEM((1024, 2048), BF),
            pltpu.VMEM((2, 8, 1024, 256), BF),
            pltpu.VMEM((2, 8, 256, 1024), BF),
            pltpu.VMEM((4, 4, 2, ROWS, 1024), BF),
            pltpu.VMEM((4, 4, ROWS, 1024), BF),
            pltpu.VMEM((4, 3, ROWS, 1024), BF),
        ]
        + weight_sems()
        + [
            DMA((2, 2)), DMA((2, 2)), DMA((2,)), DMA((2,)), DMA((4, 2)), DMA((4, 2)),
            DMA((4,)), DMA((4,)), DMA((4, 3)), DMA((4, 3)), DMA((3,)), DMA((2, 4)),
        ],
        compiler_params=pltpu.CompilerParams(collective_id=3, has_side_effects=True, vmem_limit_bytes=60 * 2**20),
        name="experts",
    )(ext, hidden_state, w_up, w_down)[0]


def on_device(
    tokens,
    att_ids,
    mlp_ids,
    att_gain,
    att_in,
    att_router,
    att_out,
    mlp_gain,
    mlp_router,
    w_up,
    w_down,
):
    row_count = tokens.shape[0]
    head_width = HEADS * HDIM
    in_all, router_all = gather_att_in(att_in, att_router.T)
    normed = rms_norm(tokens, att_gain).astype(BF)
    proj = jnp.dot(normed, in_all.reshape(D, 768), preferred_element_type=F32)
    att_logit = jnp.einsum(
        "tsk,snk->tn", normed.reshape(row_count, 4, 1024), router_all, preferred_element_type=F32
    )
    query = proj[:, :head_width].astype(BF).reshape(row_count, HEADS, HDIM)
    keys = proj[:, head_width : 2 * head_width].astype(BF)
    value_all = proj[:, 2 * head_width :].reshape(row_count, HEADS, ATT_EXP, HDIM)
    chosen = jnp.sum(
        (att_ids[..., None] == jnp.arange(ATT_EXP)[None, None, None, :]).astype(F32), axis=2
    )
    att_weight = jax.nn.sigmoid(att_logit.reshape(row_count, HEADS, ATT_EXP)) * chosen
    values = jnp.sum(att_weight[..., None] * value_all, axis=2).astype(BF).reshape(row_count, head_width)
    kv_all, out_all = gather_kv(jnp.concatenate([keys, values], axis=1), att_out)
    kv_rows = kv_all.reshape(-1, 4, HDIM)
    first_row = lax.axis_index(("outer", "inner")) * row_count
    query_position = first_row + jnp.arange(row_count)
    scores = jnp.einsum("thd,shd->hts", query, kv_rows[:, :HEADS], preferred_element_type=F32) * HDIM ** (-0.5)
    visible = jnp.arange(kv_rows.shape[0])[None, None, :] <= query_position[None, :, None]
    scores = jnp.where(visible, scores, -1e30)
    weights = jnp.exp(scores - jnp.max(scores, axis=-1, keepdims=True))
    total = jnp.sum(weights, axis=-1)
    attended = jnp.einsum("hts,shd->thd", weights.astype(BF), kv_rows[:, HEADS:], preferred_element_type=F32)
    attended = attended / total.T[..., None]
    head_normed = attended * lax.rsqrt(jnp.mean(attended * attended, axis=-1, keepdims=True) + epsilon)
    mixed = (head_normed[:, :, None, :] * att_weight[..., None]).reshape(row_count, HEADS * ATT_EXP * HDIM)
    mixed = mixed.astype(BF)
    att_result = jnp.einsum("tk,skn->tsn", mixed, out_all, preferred_element_type=F32).reshape(row_count, D)
    hidden_state = tokens.astype(F32) + att_result
    mlp_in = rms_norm(hidden_state, mlp_gain).astype(BF)
    logits = jnp.dot(mlp_in, mlp_router, preferred_element_type=F32)
    picked = jnp.any(mlp_ids[..., None] == jnp.arange(mlp_router.shape[1])[None, None, :], axis=1)
    gates = jnp.where(picked, jax.nn.sigmoid(logits), 0.0)
    high = lax.reduce_precision(gates, 8, 7)
    ext = jnp.concatenate([mlp_in, high.astype(BF), (gates - high).astype(BF)], axis=1)
    return moe(ext, hidden_state, w_up, w_down)


def solution(mesh):
    in_specs = (
        P(("seq", "outer", "inner"), None),
        P(("seq", "outer", "inner"), None, None),
        P(("seq", "outer", "inner"), None),
        P(),
        P("inner", None),
        P("inner", None),
        P(None, "inner"),
        P(),
        P(),
        P(("outer", "inner"), None, None),
        P(("outer", "inner"), None, None),
    )
    out_specs = P(("seq", "outer", "inner"), None)
    return jax.shard_map(
        on_device, mesh=mesh, in_specs=in_specs, out_specs=out_specs, check_vma=False
    )
```

```python
import functools

import jax
import jax.numpy as jnp
from jax import lax
from jax.experimental import pallas as pl
from jax.experimental.pallas import tpu as pltpu
from jax.sharding import PartitionSpec as P

D = 4096
HEADS = 2
HDIM = 64
ATT_EXP = 4
EXT = D + 128
ROWS = 128
EARLY = 4
epsilon = 1e-05
MESH = pl.DeviceIdType.MESH
ANY = pl.BlockSpec(memory_space=pl.ANY)
VM = pl.BlockSpec(memory_space=pltpu.VMEM)
DMA = pltpu.SemaphoreType.DMA
BF = jnp.bfloat16
F32 = jnp.float32


class Place:
    def __init__(self):
        self.seq, self.outer, self.inner = (lax.axis_index(a) for a in ("seq", "outer", "inner"))
        self.zl, self.y = self.seq // 4, self.seq % 4
        self.x, self.c = self.outer // 2, self.outer % 2

    def along_z(self, d):
        return (self.seq, self.outer, (self.inner + d) % 4)

    def along_y(self, d):
        return (self.zl * 4 + (self.y + d) % 4, self.outer, self.inner)

    def along_x(self, d):
        return (self.seq, ((self.x + d) % 4) * 2 + self.c, self.inner)

    def sibling(self):
        return (self.seq, self.x * 2 + 1 - self.c, self.inner)

    def pair(self):
        return ((1 - self.zl) * 4 + self.y, self.outer, self.inner)

    def beyond(self):
        return ((1 - self.zl) * 4 + self.y, self.outer, (self.inner + 2 * self.zl - 1) % 4)


def meet(peers):
    barrier = pltpu.get_barrier_semaphore()
    for peer in peers:
        pl.semaphore_signal(barrier, inc=1, device_id=peer, device_id_type=MESH)
    pl.semaphore_wait(barrier, len(peers))


def remote(src, dst, send, recv, peer):
    return pltpu.make_async_remote_copy(
        src_ref=src, dst_ref=dst, send_sem=send, recv_sem=recv, device_id=peer, device_id_type=MESH
    )


def spread_over_z(at, own, gathered, full, p, sems):
    s1, r1, s2, r2, s3, r3 = sems
    n = full // 16
    spans = (
        pl.ds(pl.multiple_of(p.c * (4 * n) + p.y * n, n), n),
        pl.ds(pl.multiple_of(8 * n + p.c * (4 * n) + p.x * n, n), n),
    )
    halves = tuple(pl.ds(pl.multiple_of(8 * n * h + p.c * (4 * n), 4 * n), 4 * n) for h in range(2))

    def first(d, h):
        return remote(
            own.at[spans[h]], gathered.at[p.inner, spans[h]], s1.at[at, d - 1, h], r1.at[at, d - 1, h], p.along_z(d)
        )

    def second(d, h, e):
        j = (p.inner - d + 4) % 4
        peer = p.along_y(e) if h == 0 else p.along_x(e)
        block = gathered.at[j, spans[h]]
        return remote(block, block, s2.at[at, d - 1, h, e - 1], r2.at[at, d - 1, h, e - 1], peer)

    def third(d, h):
        j = (p.inner - d + 4) % 4
        block = gathered.at[j, halves[h]]
        return remote(block, block, s3.at[at, d - 1, h], r3.at[at, d - 1, h], p.sibling())

    order = (1, 3, 2)
    every = [(d, h) for d in order for h in range(2)]

    def go1():
        for d, h in every:
            first(d, h).start()

    def go2(d):
        for h in range(2):
            first(d, h).wait_recv()
            for e in (1, 3, 2):
                second(d, h, e).start()

    def go3(d):
        for h in range(2):
            for e in (1, 3, 2):
                second(d, h, e).wait_recv()
            third(d, h).start()

    def arrived():
        for d, h in every:
            third(d, h).wait_recv()

    def sent():
        for d, h in every:
            first(d, h).wait_send()
            third(d, h).wait_send()
            for e in (1, 3, 2):
                second(d, h, e).wait_send()

    return order, go1, go2, go3, arrived, sent


def spread_sems(n):
    return [DMA((n, 3, 2)), DMA((n, 3, 2)), DMA((n, 3, 2, 3)), DMA((n, 3, 2, 3)), DMA((n, 3, 2)), DMA((n, 3, 2))]


def square_peers(p):
    return (
        [p.along_z(d) for d in (1, 2, 3)]
        + [p.along_y(d) for d in (1, 2, 3)]
        + [p.along_x(d) for d in (1, 2, 3)]
        + [p.sibling()]
    )


class Weights:
    def __init__(self, p, steps, sems):
        self.p, self.steps = p, steps
        self.ns, self.fr, self.ps, self.sr, self.ys, self.yr = sems
        self.k = p.y % 2
        self.way = 2 * p.zl - 1
        self.done = 0

    def part(self, ref, up, e, c):
        span = pl.ds(pl.multiple_of(c * 256, 256), 256)
        return ref.at[e, span, :] if up else ref.at[e, :, span]

    def chunk(self, i, shard, c):
        _, gathered, up, _, base = self.steps[i]
        return self.part(gathered, up, ((shard + 8) % 4) * 2 + self.k, base + c)

    def to_next(self, i, t):
        p = self.p
        own, _, up, base, _ = self.steps[i]
        if t < 2:
            src = self.part(own, up, self.k, base + t)
            dst = self.chunk(i, p.inner, t)
        else:
            src = dst = self.chunk(i, p.inner - self.way, 1 - p.zl)
        return remote(src, dst, self.ns.at[i, t], self.fr.at[i, t], p.beyond())

    def far(self, t):
        p = self.p
        return (p.inner + self.way, t) if t < 2 else (p.inner + 2, p.zl)

    def near(self, t):
        p = self.p
        return (p.inner - self.way, t) if t < 2 else (p.inner + 2, 1 - p.zl)

    def forward(self, i, t):
        block = self.chunk(i, *self.far(t))
        return remote(block, block, self.ps.at[i, t], self.sr.at[i, t], self.p.pair())

    def sideways(self, i, t, which):
        shard, c = (self.far, self.near)[which](t)
        block = self.chunk(i, shard, c)
        peer = self.p.along_y(5 - 2 * (c % 2))
        return remote(block, block, self.ys.at[i, t, which], self.yr.at[i, t, which], peer)

    def begin(self, i):
        for t in range(2):
            self.to_next(i, t).start()

    def take_far(self, i, t):
        self.to_next(i, t).wait_recv()
        self.forward(i, t).start()
        self.sideways(i, t, 0).start()

    def take_near(self, i, t):
        self.forward(i, t).wait_recv()
        self.sideways(i, t, 1).start()

    def turn(self, i):
        n = len(self.steps)
        if i < n - 1:
            self.begin(i + 1)
        if i < n:
            self.take_far(i, 0)
            self.take_far(i, 1)
        if 0 <= i - 2 < n:
            self.take_far(i - 2, 2)
        if 0 <= i - 1 < n:
            self.take_near(i - 1, 0)
            self.take_near(i - 1, 1)
            self.to_next(i - 1, 2).start()
        if 0 <= i - 3 < n:
            self.take_near(i - 3, 2)

    def advance(self, to):
        for i in range(self.done, min(max(to, self.done) + 1, len(self.steps) + 3)):
            self.turn(i)
            self.done = i + 1

    def settle(self, i):
        for t in range(3):
            for which in range(2):
                self.sideways(i, t, which).wait_recv()

    def drain(self):
        for i in range(len(self.steps)):
            for t in range(3):
                self.to_next(i, t).wait_send()
                self.forward(i, t).wait_send()
                for which in range(2):
                    self.sideways(i, t, which).wait_send()

    def peers(self):
        p = self.p
        return [p.beyond(), p.pair(), p.along_y(1), p.along_y(3)]


def weight_sems(n):
    return [DMA((n, 3))] * 4 + [DMA((n, 3, 2))] * 2


def across_rows(a, b):
    return lax.dot_general(a, b, (((1,), (1,)), ((), ())), preferred_element_type=F32)


def norm_rows(src, gain, dst):
    def one(r, carry):
        rows = pl.ds(pl.multiple_of(16 * r, 16), 16)
        floats = src[rows, :].astype(F32)
        scale = lax.rsqrt(jnp.mean(floats * floats, axis=-1, keepdims=True) + epsilon)
        dst[rows, 0:D] = (floats * scale * gain[...]).astype(BF)
        return carry

    lax.fori_loop(0, 8, one, 0)


def attention_kernel(
    tok, gain, mlp_gain, chosen, picked, mlp_router, w_in, router, w_out, up, ext, hs, gup,
    normed, gw, gr, kv, gk, ao,
    s1, r1, s2, r2, s3, r3, ro_s, ro_r, sz, rz, sx, rx, sc, rc, local, ns, fr, ps, sr, ys, yr,
):
    p = Place()
    steps = [(up, gup, True, 2 * m, 2 * m) for m in range(2 * EARLY)]
    w = Weights(p, steps, (ns, fr, ps, sr, ys, yr))
    own = [
        pltpu.make_async_copy(w_in, gw.at[p.inner], local.at[0]),
        pltpu.make_async_copy(router, gr.at[p.inner], local.at[1]),
        pltpu.make_async_copy(w_out, ao.at[p.inner], local.at[2]),
    ]
    for copy in own:
        copy.start()
    meet(square_peers(p) + [p.beyond(), p.pair()])
    sems = (s1, r1, s2, r2, s3, r3)
    order, in1, in2, in3, in_arrived, in_sent = spread_over_z(0, w_in, gw, 1024, p, sems)
    _, out1, out2, out3, out_arrived, out_sent = spread_over_z(1, w_out, ao, 512, p, sems)
    routers = [remote(router, gr.at[p.inner], ro_s.at[d - 1], ro_r.at[d - 1], p.along_z(d)) for d in (1, 2, 3)]
    zs = [remote(kv, gk.at[p.outer, p.inner], sz.at[d - 1], rz.at[d - 1], p.along_z(d)) for d in (1, 2, 3)]
    xs = [remote(gk.at[p.outer], gk.at[p.outer], sx.at[d - 1], rx.at[d - 1], p.along_x(d)) for d in (1, 2, 3)]
    cs = []
    for d in range(4):
        o = ((p.x - d + 4) % 4) * 2 + p.c
        cs.append(remote(gk.at[o], gk.at[o], sc.at[d], rc.at[d], p.sibling()))

    in1()
    for copy in routers:
        copy.start()
    norm_rows(tok, gain, normed)
    for d in order:
        in2(d)
    w.begin(0)
    for d in order:
        in3(d)
    w.advance(0)
    in_arrived()
    w.advance(1)
    for copy in routers:
        copy.wait_recv()
    own[0].wait()
    own[1].wait()

    proj = jnp.zeros((ROWS, 768), F32)
    logit = jnp.zeros((ROWS, 8), F32)
    for j in range(4):
        piece = normed[:, 1024 * j : 1024 * (j + 1)]
        proj += jnp.dot(piece, gw[j], preferred_element_type=F32)
        logit += across_rows(piece, gr[j])
    weight = jax.nn.sigmoid(logit) * chosen[...]
    mixes = []
    for h in range(HEADS):
        mix = jnp.zeros((ROWS, HDIM), F32)
        for e in range(4 * h, 4 * h + 4):
            mix += weight[:, e : e + 1] * proj[:, 256 + HDIM * e : 256 + HDIM * (e + 1)]
        mixes.append(mix)
    kv[:, 0:128] = proj[:, 128:256].astype(BF)
    kv[:, 128:256] = jnp.concatenate(mixes, axis=1).astype(BF)
    query = proj[:, 0:128].astype(BF)
    for copy in zs:
        copy.start()
    keep = pltpu.make_async_copy(kv, gk.at[p.outer, p.inner], local.at[3])
    keep.start()
    out1()
    w.advance(2)
    keep.wait()
    for copy in zs:
        copy.wait_recv()
    for copy in (xs[0], xs[2], xs[1]):
        copy.start()
    cs[0].start()
    for d in order:
        out2(d)
    w.advance(3)
    for d in (1, 3, 2):
        xs[d - 1].wait_recv()
        cs[d].start()
    for d in order:
        out3(d)
    w.advance(4)
    for copy in cs:
        copy.wait_recv()

    place = (p.outer * 4 + p.inner) * ROWS + lax.broadcasted_iota(jnp.int32, (ROWS, 512), 0)
    spot = lax.broadcasted_iota(jnp.int32, (ROWS, 512), 1)
    heads = []
    for h in range(HEADS):
        mine = query[:, HDIM * h : HDIM * (h + 1)]

        def one(o, carry):
            top, total, out = carry
            held = gk[o].reshape(512, 256)
            scores = across_rows(mine, held[:, HDIM * h : HDIM * (h + 1)]) * HDIM ** (-0.5)
            scores = jnp.where(spot + 512 * o <= place, scores, -1e30)
            high = jnp.maximum(top, jnp.max(scores, axis=-1, keepdims=True))
            shares = jnp.exp(scores - high)
            fade = jnp.exp(top - high)
            values = held[:, 128 + HDIM * h : 128 + HDIM * (h + 1)]
            return (
                high,
                total * fade + jnp.sum(shares, axis=-1, keepdims=True),
                out * fade + jnp.dot(shares.astype(BF), values, preferred_element_type=F32),
            )

        start = (
            jnp.full((ROWS, 1), -1e30, F32),
            jnp.zeros((ROWS, 1), F32),
            jnp.zeros((ROWS, HDIM), F32),
        )
        _, total, out = lax.fori_loop(0, p.outer + 1, one, start)
        out = out / total
        heads.append(out * lax.rsqrt(jnp.mean(out * out, axis=-1, keepdims=True) + epsilon))
        w.advance(0)
    mixed = jnp.concatenate([weight[:, e : e + 1] * heads[e // 4] for e in range(8)], axis=1).astype(BF)
    out_arrived()
    own[2].wait()
    for j in range(4):
        span = slice(1024 * j, 1024 * (j + 1))
        hs[:, span] = tok[:, span].astype(F32) + jnp.dot(mixed, ao[j], preferred_element_type=F32)
    w.advance(0)
    norm_rows(hs, mlp_gain, ext)
    gates = jax.nn.sigmoid(across_rows(ext[:, 0:D], mlp_router[...])) * picked[...]
    high = gates.astype(BF)
    ext[:, D:] = jnp.concatenate([high, (gates - high.astype(F32)).astype(BF)], axis=1)
    w.advance(99)
    for i in range(2 * EARLY):
        w.settle(i)
    w.drain()
    in_sent()
    out_sent()
    for copy in routers + zs + xs + cs:
        copy.wait_send()


def attention(*arrays):
    return pl.pallas_call(
        attention_kernel,
        out_shape=(
            jax.ShapeDtypeStruct((ROWS, EXT), BF),
            jax.ShapeDtypeStruct((ROWS, D), F32),
            jax.ShapeDtypeStruct((8, EARLY * 1024, 256), BF),
        ),
        in_specs=[VM] * 6 + [ANY] * 4,
        out_specs=(VM, VM, ANY),
        scratch_shapes=[
            pltpu.VMEM((ROWS, D), BF),
            pltpu.VMEM((4, 1024, 768), BF),
            pltpu.VMEM((4, 8, 1024), BF),
            pltpu.VMEM((ROWS, 256), BF),
            pltpu.VMEM((8, 4, ROWS, 256), BF),
            pltpu.VMEM((4, 512, 1024), BF),
        ]
        + spread_sems(2)
        + [DMA((3,))] * 6
        + [DMA((4,))] * 3
        + weight_sems(2 * EARLY),
        compiler_params=pltpu.CompilerParams(collective_id=1, has_side_effects=True, vmem_limit_bytes=60 * 2**20),
        name="attention",
    )(*arrays)


def moe_kernel(
    ext, hs, up, early, down, out, late, gdn,
    xall, acc, hid, wbuf, dbuf, part, pairbuf, xbuf,
    ns, fr, ps, sr, ys, yr, ts, tr, us, ur, vs, vr, es, er, qs, qr, local, load,
):
    p = Place()
    steps = [(up, late, True, 2 * m, 2 * m - 4 * EARLY) for m in range(2 * EARLY, 8)]
    steps += [(down, gdn, False, 2 * m, 2 * m) for m in range(8)]
    w = Weights(p, steps, (ns, fr, ps, sr, ys, yr))
    meet(w.peers() + [p.along_x(1), p.along_x(2), p.along_x(3), p.sibling()])
    def rows(o, h):
        return xall.at[o, pl.ds(64 * h, 64), :]

    def block(d):
        return ((p.x + d) % 4) * 2 + p.c

    def mine(d, h):
        src = ext.at[pl.ds(64 * h, 64), :]
        return remote(src, rows(p.outer, h), ts.at[(d - 1) // 2, h], tr.at[(d - 1) // 2, h], p.along_x(d))

    def relay(d):
        h = (d - 1) // 2
        src = rows(block(4 - d), h)
        return remote(src, src, us.at[h], ur.at[h], p.along_x(d))

    def across(d, h):
        src = ext.at[pl.ds(64 * h, 64), :] if d == 0 else rows(block(d), h)
        return remote(src, rows(block(d), h), vs.at[d, h], vr.at[d, h], p.sibling())

    for h in range(2):
        for d in (1, 3):
            mine(d, h if d == 1 else 1 - h).start()
    for h in range(2):
        across(0, h).start()
    keep = pltpu.make_async_copy(ext, xall.at[p.outer], local.at[2])
    keep.start()
    w.begin(0)

    def loads(own, gathered, buffer, at):
        for d in range(4):
            two = pl.ds(2 * ((p.inner + d) % 4), 2)
            src = own if d == 0 else gathered.at[two]
            yield pltpu.make_async_copy(src, buffer.at[two], load.at[at, d])

    def load_up(m):
        held, base = (early, 0) if m < EARLY else (late, EARLY)
        mine_up = up.at[:, pl.ds(1024 * m, 1024), :]
        return loads(mine_up, held.at[:, pl.ds(1024 * (m - base), 1024), :], wbuf.at[m % 3], m % 3)

    def load_down(m):
        span = pl.ds(1024 * m, 1024)
        return loads(down.at[:, :, span], gdn.at[:, :, span], dbuf.at[m % 2], 3 + m % 2)

    def fetch(copies):
        for copy in copies:
            copy.start()

    def land(copies):
        for copy in copies:
            copy.wait()

    def run_up(m, groups):
        for d in groups:
            there = (p.x + d) % 4

            def one(e, carry):
                tokens = xall[pl.ds(2 * there, 2), :, pl.ds(1024 * m, 1024)].reshape(256, 1024)
                rows = pl.ds(pl.multiple_of(256 * there, 256), 256)
                got = jnp.dot(tokens, wbuf[m % 3, e], preferred_element_type=F32)
                if m == 0:
                    acc[e, rows, :] = got
                else:
                    acc[e, rows, :] += got
                return carry

            lax.fori_loop(0, 8, one, 0)

    def run_up_all(m):
        def one(e, carry):
            tokens = xall[:, :, pl.ds(1024 * m, 1024)].reshape(1024, 1024)
            acc[e] += jnp.dot(tokens, wbuf[m % 3, e], preferred_element_type=F32)
            return carry

        lax.fori_loop(0, 8, one, 0)

    def gate():
        names = lax.broadcasted_iota(jnp.int32, (128, 256), 0) % 64
        shares = xall[:, :, D:].reshape(1024, 128)

        def one(e, carry):
            pick = jnp.where(names == p.outer * 8 + e, 1.0, 0.0).astype(BF)
            scale = jnp.dot(shares, pick, preferred_element_type=F32)
            hid[:, pl.ds(pl.multiple_of(256 * e, 256), 256)] = (jnp.maximum(acc[e], 0.0) * scale).astype(BF)
            return carry

        lax.fori_loop(0, 8, one, 0)

    def run_down(m):
        def one(n, carry):
            span = pl.ds(pl.multiple_of(256 * n, 256), 256)
            weights = dbuf[m % 2, :, :, span].reshape(2048, 256)
            got = jnp.dot(hid[...], weights, preferred_element_type=F32)
            part[m, :, :, :, span] = got.astype(BF).reshape(4, 2, 128, 256)
            return carry

        lax.fori_loop(0, 4, one, 0)

    def swap(m):
        return remote(part.at[m, :, 1 - p.c], pairbuf.at[m], es.at[m], er.at[m], p.sibling())

    def give(m, d):
        there = (p.x + d) % 4
        return remote(part.at[m, there, p.c], xbuf.at[m, d - 1], qs.at[m, d - 1], qr.at[m, d - 1], p.along_x(d))

    def add_pair(m):
        swap(m).wait_recv()
        for d in (1, 3, 2):
            there = (p.x + d) % 4
            total = part[m, there, p.c].astype(F32) + pairbuf[m, there].astype(F32)
            part[m, there, p.c] = total.astype(BF)
            give(m, d).start()

    def finish(m):
        span = pl.ds(1024 * m, 1024)
        total = hs[:, span] + part[m, p.x, p.c].astype(F32) + pairbuf[m, p.x].astype(F32)
        for d in (1, 3, 2):
            give(m, d).wait_recv()
            total += xbuf[m, d - 1].astype(F32)
        out[:, span] = total.astype(BF)

    def from_sibling(d):
        for h in range(2):
            across(d, h).wait_recv()

    def part_0():
        mine(1, 0).wait_recv()
        relay(1).start()
        mine(3, 1).wait_recv()
        relay(3).start()
        across(3, 0).start()
        across(1, 1).start()
        keep.wait()
        from_sibling(0)
        for m in range(2):
            land(load_up(m))
            run_up(m, (0,))

    def part_1():
        mine(1, 1).wait_recv()
        across(3, 1).start()
        mine(3, 0).wait_recv()
        across(1, 0).start()
        from_sibling(1)
        from_sibling(3)
        for m in range(2):
            run_up(m, (1, 3))

    def part_2():
        for d in (1, 3):
            relay(d).wait_recv()
            across(2, (d - 1) // 2).start()
        if EARLY > 2:
            fetch(load_up(2))
        from_sibling(2)
        for m in range(2):
            run_up(m, (2,))
        if EARLY > 3:
            fetch(load_up(3))

    def rest_up(m):
        if m >= EARLY:
            w.settle(2 * (m - EARLY))
            w.settle(2 * (m - EARLY) + 1)
            fetch(load_up(m))
        land(load_up(m))
        run_up_all(m)
        if m == 3:
            gate()

    def produce(m):
        w.settle(2 * (4 - EARLY + m))
        w.settle(2 * (4 - EARLY + m) + 1)
        fetch(load_down(m))
        if m > 0:
            add_pair(m - 1)
        if m > 1:
            finish(m - 2)
        land(load_down(m))
        run_down(m)
        swap(m).start()

    fetch(load_up(0))
    fetch(load_up(1))
    w.advance(0)
    part_0()
    w.advance(2)
    part_1()
    w.advance(3)
    part_2()
    for m in (2, 3):
        w.advance(2 * (m - EARLY) + 4 if m >= EARLY else 0)
        rest_up(m)
    for m in range(4):
        w.advance(2 * (4 - EARLY + m) + 4)
        produce(m)
    add_pair(3)
    finish(2)
    finish(3)
    w.drain()
    for h in range(2):
        for d in (1, 3):
            mine(d, h).wait_send()
        for d in range(4):
            across(d, h).wait_send()
    for d in (1, 3):
        relay(d).wait_send()
    for m in range(4):
        swap(m).wait_send()
        for d in (1, 2, 3):
            give(m, d).wait_send()


def moe(ext, hidden_state, w_up, gathered_up, w_down):
    return pl.pallas_call(
        moe_kernel,
        out_shape=(
            jax.ShapeDtypeStruct((ROWS, D), BF),
            jax.ShapeDtypeStruct((8, max(1, 4 - EARLY) * 1024, 256), BF),
            jax.ShapeDtypeStruct((8, 256, D), BF),
        ),
        in_specs=[ANY, VM, ANY, ANY, ANY],
        out_specs=(VM, ANY, ANY),
        scratch_shapes=[
            pltpu.VMEM((8, ROWS, EXT), BF),
            pltpu.VMEM((8, 1024, 256), F32),
            pltpu.VMEM((1024, 2048), BF),
            pltpu.VMEM((3, 8, 1024, 256), BF),
            pltpu.VMEM((2, 8, 256, 1024), BF),
            pltpu.VMEM((4, 4, 2, ROWS, 1024), BF),
            pltpu.VMEM((4, 4, ROWS, 1024), BF),
            pltpu.VMEM((4, 3, ROWS, 1024), BF),
        ]
        + weight_sems(16 - 2 * EARLY)
        + [
            DMA((2, 2)), DMA((2, 2)), DMA((2,)), DMA((2,)), DMA((4, 2)), DMA((4, 2)),
            DMA((4,)), DMA((4,)), DMA((4, 3)), DMA((4, 3)), DMA((3,)), DMA((5, 4)),
        ],
        compiler_params=pltpu.CompilerParams(collective_id=3, has_side_effects=True, vmem_limit_bytes=60 * 2**20),
        name="experts",
    )(ext, hidden_state, w_up, gathered_up, w_down)[0]


def on_device(
    tokens,
    att_ids,
    mlp_ids,
    att_gain,
    att_in,
    att_router,
    att_out,
    mlp_gain,
    mlp_router,
    w_up,
    w_down,
):
    row_count = tokens.shape[0]
    chosen = jnp.any(att_ids[..., None] == jnp.arange(ATT_EXP)[None, None, None, :], axis=2)
    picked = jnp.any(mlp_ids[..., None] == jnp.arange(mlp_router.shape[1])[None, None, :], axis=1)
    ext, hidden_state, gathered_up = attention(
        tokens,
        att_gain[None, :],
        mlp_gain[None, :],
        chosen.reshape(row_count, HEADS * ATT_EXP).astype(F32),
        picked.astype(F32),
        mlp_router.T,
        att_in,
        att_router.T,
        att_out,
        w_up,
    )
    return moe(ext, hidden_state, w_up, gathered_up, w_down)


def solution(mesh):
    in_specs = (
        P(("seq", "outer", "inner"), None),
        P(("seq", "outer", "inner"), None, None),
        P(("seq", "outer", "inner"), None),
        P(),
        P("inner", None),
        P("inner", None),
        P(None, "inner"),
        P(),
        P(),
        P(("outer", "inner"), None, None),
        P(("outer", "inner"), None, None),
    )
    out_specs = P(("seq", "outer", "inner"), None)
    return jax.shard_map(
        on_device, mesh=mesh, in_specs=in_specs, out_specs=out_specs, check_vma=False
    )
```

```python
import functools

import jax
import jax.numpy as jnp
from jax import lax
from jax.experimental import pallas as pl
from jax.experimental.pallas import tpu as pltpu
from jax.sharding import PartitionSpec as P

D = 4096
HEADS = 2
HDIM = 64
ATT_EXP = 4
EXT = D + 128
ROWS = 128
SLOT = {0: 0, 1: 1, 3: 2, 2: 3}
epsilon = 1e-05
MESH = pl.DeviceIdType.MESH
ANY = pl.BlockSpec(memory_space=pl.ANY)
VM = pl.BlockSpec(memory_space=pltpu.VMEM)
DMA = pltpu.SemaphoreType.DMA
BF = jnp.bfloat16
F32 = jnp.float32


class Place:
    def __init__(self):
        self.seq, self.outer, self.inner = (lax.axis_index(a) for a in ("seq", "outer", "inner"))
        self.zl, self.y = self.seq // 4, self.seq % 4
        self.x, self.c = self.outer // 2, self.outer % 2

    def along_z(self, d):
        return (self.seq, self.outer, (self.inner + d) % 4)

    def along_y(self, d):
        return (self.zl * 4 + (self.y + d) % 4, self.outer, self.inner)

    def along_x(self, d):
        return (self.seq, ((self.x + d) % 4) * 2 + self.c, self.inner)

    def sibling(self):
        return (self.seq, self.x * 2 + 1 - self.c, self.inner)

    def pair(self):
        return ((1 - self.zl) * 4 + self.y, self.outer, self.inner)

    def beyond(self):
        return ((1 - self.zl) * 4 + self.y, self.outer, (self.inner + 2 * self.zl - 1) % 4)


def meet(peers):
    barrier = pltpu.get_barrier_semaphore()
    for peer in peers:
        pl.semaphore_signal(barrier, inc=1, device_id=peer, device_id_type=MESH)
    pl.semaphore_wait(barrier, len(peers))


def remote(src, dst, send, recv, peer):
    return pltpu.make_async_remote_copy(
        src_ref=src, dst_ref=dst, send_sem=send, recv_sem=recv, device_id=peer, device_id_type=MESH
    )


def spread_over_z(at, own, gathered, bands, p, sems):
    s1, r1, s2, r2, s3, r3, s4, r4 = sems

    def span(h, size):
        base, n, y_first = bands[h]
        outer, inner = (p.x, p.y) if y_first else (p.y, p.x)
        row = base + p.c * 16 * n + (outer * 4 * n if size < 16 else 0) + (inner * n if size < 4 else 0)
        return pl.ds(pl.multiple_of(row, n), size * n)

    def first(d, h):
        piece = span(h, 1)
        return remote(own.at[piece], gathered.at[p.inner, piece], s1.at[at, d - 1, h], r1.at[at, d - 1, h], p.along_z(d))

    def second(d, h, e):
        block = gathered.at[(p.inner - d + 4) % 4, span(h, 1)]
        peer = p.along_y(e) if bands[h][2] else p.along_x(e)
        return remote(block, block, s2.at[at, d - 1, h, e - 1], r2.at[at, d - 1, h, e - 1], peer)

    def third(d, h, e):
        block = gathered.at[(p.inner - d + 4) % 4, span(h, 4)]
        peer = p.along_x(e) if bands[h][2] else p.along_y(e)
        return remote(block, block, s3.at[at, d - 1, h, e - 1], r3.at[at, d - 1, h, e - 1], peer)

    def fourth(d, h):
        block = gathered.at[(p.inner - d + 4) % 4, span(h, 16)]
        return remote(block, block, s4.at[at, d - 1, h], r4.at[at, d - 1, h], p.sibling())

    order = (1, 3, 2)
    every = [(d, h) for d in order for h in range(len(bands))]

    def go1():
        for d, h in every:
            first(d, h).start()

    def go2():
        for d, h in every:
            first(d, h).wait_recv()
            for e in order:
                second(d, h, e).start()

    def go3():
        for d, h in every:
            for e in order:
                second(d, h, e).wait_recv()
            for e in order:
                third(d, h, e).start()

    def go4():
        for d, h in every:
            for e in order:
                third(d, h, e).wait_recv()
            fourth(d, h).start()

    def arrived():
        for d, h in every:
            fourth(d, h).wait_recv()

    def sent():
        for d, h in every:
            first(d, h).wait_send()
            fourth(d, h).wait_send()
            for e in order:
                second(d, h, e).wait_send()
                third(d, h, e).wait_send()

    return go1, go2, go3, go4, arrived, sent


def spread_sems(n):
    return [DMA((n, 3, 2))] * 2 + [DMA((n, 3, 2, 3))] * 4 + [DMA((n, 3, 2))] * 2


def square_peers(p):
    return (
        [p.along_z(d) for d in (1, 2, 3)]
        + [p.along_y(d) for d in (1, 2, 3)]
        + [p.along_x(d) for d in (1, 2, 3)]
        + [p.sibling()]
    )


class Weights:
    def __init__(self, p, steps, sems):
        self.p, self.steps = p, steps
        self.ns, self.fr, self.ps, self.sr, self.ys, self.yr = sems
        self.k = p.y % 2
        self.way = 2 * p.zl - 1
        self.done = 0

    def part(self, ref, up, e, c):
        span = pl.ds(pl.multiple_of(c * 256, 256), 256)
        return ref.at[e, span, :] if up else ref.at[e, :, span]

    def chunk(self, i, shard, c):
        _, gathered, up, _, base = self.steps[i]
        return self.part(gathered, up, ((shard + 8) % 4) * 2 + self.k, base + c)

    def to_next(self, i, t):
        p = self.p
        own, _, up, base, _ = self.steps[i]
        if t < 2:
            src = self.part(own, up, self.k, base + t)
            dst = self.chunk(i, p.inner, t)
        else:
            src = dst = self.chunk(i, p.inner - self.way, 1 - p.zl)
        return remote(src, dst, self.ns.at[i, t], self.fr.at[i, t], p.beyond())

    def far(self, t):
        p = self.p
        return (p.inner + self.way, t) if t < 2 else (p.inner + 2, p.zl)

    def near(self, t):
        p = self.p
        return (p.inner - self.way, t) if t < 2 else (p.inner + 2, 1 - p.zl)

    def forward(self, i, t):
        block = self.chunk(i, *self.far(t))
        return remote(block, block, self.ps.at[i, t], self.sr.at[i, t], self.p.pair())

    def sideways(self, i, t, which):
        shard, c = (self.far, self.near)[which](t)
        block = self.chunk(i, shard, c)
        peer = self.p.along_y(5 - 2 * (c % 2))
        return remote(block, block, self.ys.at[i, t, which], self.yr.at[i, t, which], peer)

    def begin(self, i):
        for t in range(2):
            self.to_next(i, t).start()

    def take_far(self, i, t):
        self.to_next(i, t).wait_recv()
        self.forward(i, t).start()
        self.sideways(i, t, 0).start()

    def take_near(self, i, t):
        self.forward(i, t).wait_recv()
        self.sideways(i, t, 1).start()

    def turn(self, i):
        n = len(self.steps)
        if i < n - 1:
            self.begin(i + 1)
        if i < n:
            self.take_far(i, 0)
            self.take_far(i, 1)
        if 0 <= i - 2 < n:
            self.take_far(i - 2, 2)
        if 0 <= i - 1 < n:
            self.take_near(i - 1, 0)
            self.take_near(i - 1, 1)
            self.to_next(i - 1, 2).start()
        if 0 <= i - 3 < n:
            self.take_near(i - 3, 2)

    def advance(self, to):
        for i in range(self.done, min(max(to, self.done) + 1, len(self.steps) + 3)):
            self.turn(i)
            self.done = i + 1

    def settle(self, i):
        for t in range(3):
            for which in range(2):
                self.sideways(i, t, which).wait_recv()

    def drain(self):
        for i in range(len(self.steps)):
            for t in range(3):
                self.to_next(i, t).wait_send()
                self.forward(i, t).wait_send()
                for which in range(2):
                    self.sideways(i, t, which).wait_send()

    def peers(self):
        p = self.p
        return [p.beyond(), p.pair(), p.along_y(1), p.along_y(3)]


def weight_sems(n):
    return [DMA((n, 3))] * 4 + [DMA((n, 3, 2))] * 2


def across_rows(a, b):
    return lax.dot_general(a, b, (((1,), (1,)), ((), ())), preferred_element_type=F32)


def norm_rows(src, gain, dst):
    def one(r, carry):
        rows = pl.ds(pl.multiple_of(16 * r, 16), 16)
        floats = src[rows, :].astype(F32)
        scale = lax.rsqrt(jnp.mean(floats * floats, axis=-1, keepdims=True) + epsilon)
        dst[rows, 0:D] = (floats * scale * gain[...]).astype(BF)
        return carry

    lax.fori_loop(0, 8, one, 0)


def attention_kernel(
    tok, gain, mlp_gain, chosen, picked, mlp_router, w_in, router, w_out, up, ext, hs, gup,
    normed, gw, gr, kv, gk, ao,
    s1, r1, s2, r2, s3, r3, s4, r4, ro_s, ro_r, sz, rz, sx, rx, sc, rc, local, ns, fr, ps, sr, ys, yr,
):
    p = Place()
    steps = [(up, gup, True, 2 * m, 2 * m) for m in range(8)]
    w = Weights(p, steps, (ns, fr, ps, sr, ys, yr))
    own = [
        pltpu.make_async_copy(w_in, gw.at[p.inner], local.at[0]),
        pltpu.make_async_copy(router, gr.at[p.inner], local.at[1]),
        pltpu.make_async_copy(w_out, ao.at[p.inner], local.at[2]),
    ]
    for copy in own:
        copy.start()
    meet(square_peers(p) + [p.beyond(), p.pair()])
    sems = (s1, r1, s2, r2, s3, r3, s4, r4)
    in1, in2, in3, in4, in_arrived, in_sent = spread_over_z(0, w_in, gw, ((0, 16, False), (512, 16, True)), p, sems)
    out1, out2, out3, out4, out_arrived, out_sent = spread_over_z(1, w_out, ao, ((0, 16, True),), p, sems)
    routers = [remote(router, gr.at[p.inner], ro_s.at[d - 1], ro_r.at[d - 1], p.along_z(d)) for d in (1, 2, 3)]
    zs = [remote(kv, gk.at[p.outer, p.inner], sz.at[d - 1], rz.at[d - 1], p.along_z(d)) for d in (1, 2, 3)]
    xs = [remote(gk.at[p.outer], gk.at[p.outer], sx.at[d - 1], rx.at[d - 1], p.along_x(d)) for d in (1, 2, 3)]
    cs = []
    for d in range(4):
        o = ((p.x - d + 4) % 4) * 2 + p.c
        cs.append(remote(gk.at[o], gk.at[o], sc.at[d], rc.at[d], p.sibling()))

    in1()
    for copy in routers:
        copy.start()
    w.begin(0)
    norm_rows(tok, gain, normed)
    in2()
    w.advance(0)
    in3()
    w.advance(1)
    in4()
    w.advance(2)
    in_arrived()
    for copy in routers:
        copy.wait_recv()
    own[0].wait()
    own[1].wait()

    proj = jnp.zeros((ROWS, 768), F32)
    logit = jnp.zeros((ROWS, 8), F32)
    for j in range(4):
        piece = normed[:, 1024 * j : 1024 * (j + 1)]
        proj += jnp.dot(piece, gw[j], preferred_element_type=F32)
        logit += across_rows(piece, gr[j])
    weight = jax.nn.sigmoid(logit) * chosen[...]
    mixes = []
    for h in range(HEADS):
        mix = jnp.zeros((ROWS, HDIM), F32)
        for e in range(4 * h, 4 * h + 4):
            mix += weight[:, e : e + 1] * proj[:, 256 + HDIM * e : 256 + HDIM * (e + 1)]
        mixes.append(mix)
    kv[:, 0:128] = proj[:, 128:256].astype(BF)
    kv[:, 128:256] = jnp.concatenate(mixes, axis=1).astype(BF)
    query = proj[:, 0:128].astype(BF)
    for copy in zs:
        copy.start()
    keep = pltpu.make_async_copy(kv, gk.at[p.outer, p.inner], local.at[3])
    keep.start()
    out1()
    w.advance(3)
    keep.wait()
    for copy in zs:
        copy.wait_recv()
    for copy in (xs[0], xs[2], xs[1]):
        copy.start()
    cs[0].start()
    out2()
    w.advance(4)
    out3()
    for d in (1, 3, 2):
        xs[d - 1].wait_recv()
        cs[d].start()
    w.advance(5)
    out4()
    for copy in cs:
        copy.wait_recv()

    place = (p.outer * 4 + p.inner) * ROWS + lax.broadcasted_iota(jnp.int32, (ROWS, 512), 0)
    spot = lax.broadcasted_iota(jnp.int32, (ROWS, 512), 1)
    heads = []
    for h in range(HEADS):
        mine = query[:, HDIM * h : HDIM * (h + 1)]

        def one(o, carry):
            top, total, out = carry
            held = gk[o].reshape(512, 256)
            scores = across_rows(mine, held[:, HDIM * h : HDIM * (h + 1)]) * HDIM ** (-0.5)
            scores = jnp.where(spot + 512 * o <= place, scores, -1e30)
            high = jnp.maximum(top, jnp.max(scores, axis=-1, keepdims=True))
            shares = jnp.exp(scores - high)
            fade = jnp.exp(top - high)
            values = held[:, 128 + HDIM * h : 128 + HDIM * (h + 1)]
            return (
                high,
                total * fade + jnp.sum(shares, axis=-1, keepdims=True),
                out * fade + jnp.dot(shares.astype(BF), values, preferred_element_type=F32),
            )

        start = (
            jnp.full((ROWS, 1), -1e30, F32),
            jnp.zeros((ROWS, 1), F32),
            jnp.zeros((ROWS, HDIM), F32),
        )
        _, total, out = lax.fori_loop(0, p.outer + 1, one, start)
        out = out / total
        heads.append(out * lax.rsqrt(jnp.mean(out * out, axis=-1, keepdims=True) + epsilon))
        w.advance(0)
    mixed = jnp.concatenate([weight[:, e : e + 1] * heads[e // 4] for e in range(8)], axis=1).astype(BF)
    out_arrived()
    own[2].wait()
    for j in range(4):
        span = slice(1024 * j, 1024 * (j + 1))
        hs[:, span] = tok[:, span].astype(F32) + jnp.dot(mixed, ao[j], preferred_element_type=F32)
    w.advance(0)
    norm_rows(hs, mlp_gain, ext)
    gates = jax.nn.sigmoid(across_rows(ext[:, 0:D], mlp_router[...])) * picked[...]
    high = gates.astype(BF)
    ext[:, D:] = jnp.concatenate([high, (gates - high.astype(F32)).astype(BF)], axis=1)
    w.advance(99)
    for i in range(8):
        w.settle(i)
    w.drain()
    in_sent()
    out_sent()
    for copy in routers + zs + xs + cs:
        copy.wait_send()


def attention(*arrays):
    return pl.pallas_call(
        attention_kernel,
        out_shape=(
            jax.ShapeDtypeStruct((ROWS, EXT), BF),
            jax.ShapeDtypeStruct((ROWS, D), F32),
            jax.ShapeDtypeStruct((8, D, 256), BF),
        ),
        in_specs=[VM] * 6 + [ANY] * 4,
        out_specs=(VM, VM, ANY),
        scratch_shapes=[
            pltpu.VMEM((ROWS, D), BF),
            pltpu.VMEM((4, 1024, 768), BF),
            pltpu.VMEM((4, 8, 1024), BF),
            pltpu.VMEM((ROWS, 256), BF),
            pltpu.VMEM((8, 4, ROWS, 256), BF),
            pltpu.VMEM((4, 512, 1024), BF),
        ]
        + spread_sems(2)
        + [DMA((3,))] * 6
        + [DMA((4,))] * 3
        + weight_sems(8),
        compiler_params=pltpu.CompilerParams(collective_id=1, has_side_effects=True, vmem_limit_bytes=60 * 2**20),
        name="attention",
    )(*arrays)


def moe_kernel(
    ext, hs, up, early, down, out, gdn,
    xall, acc, hid, wbuf, dbuf, part, pairbuf, xbuf,
    ns, fr, ps, sr, ys, yr, ts, tr, us, ur, vs, vr, es, er, qs, qr, local, load,
):
    p = Place()
    steps = [(down, gdn, False, 2 * m, 2 * m) for m in range(8)]
    w = Weights(p, steps, (ns, fr, ps, sr, ys, yr))
    meet(w.peers() + [p.along_x(1), p.along_x(2), p.along_x(3), p.sibling()])
    def rows(d, h):
        return xall.at[SLOT[d], p.c, pl.ds(64 * h, 64), :]

    def mine(d, h):
        src = ext.at[pl.ds(64 * h, 64), :]
        return remote(src, rows(4 - d, h), ts.at[(d - 1) // 2, h], tr.at[(d - 1) // 2, h], p.along_x(d))

    def relay(d):
        h = (d - 1) // 2
        return remote(rows(4 - d, h), rows(2, h), us.at[h], ur.at[h], p.along_x(d))

    def across(d, h):
        src = ext.at[pl.ds(64 * h, 64), :] if d == 0 else rows(d, h)
        return remote(src, rows(d, h), vs.at[d, h], vr.at[d, h], p.sibling())

    for h in range(2):
        for d in (1, 3):
            mine(d, h if d == 1 else 1 - h).start()
    for h in range(2):
        across(0, h).start()
    keep = pltpu.make_async_copy(ext, xall.at[0, p.c], local.at[2])
    keep.start()
    w.begin(0)

    def loads(own, gathered, buffer, at):
        for d in range(4):
            two = pl.ds(2 * ((p.inner + d) % 4), 2)
            src = own if d == 0 else gathered.at[two]
            yield pltpu.make_async_copy(src, buffer.at[two], load.at[at, d])

    def load_up(m, slot):
        span = pl.ds(1024 * m, 1024)
        return loads(up.at[:, span, :], early.at[:, span, :], wbuf.at[slot], slot)

    def load_down(m):
        span = pl.ds(1024 * m, 1024)
        return loads(down.at[:, :, span], gdn.at[:, :, span], dbuf.at[m % 2], 3 + m % 2)

    def fetch(copies):
        for copy in copies:
            copy.start()

    def land(copies):
        for copy in copies:
            copy.wait()

    def run_up(m, slot, low, high, first):
        def one(e, carry):
            tokens = xall[low:high, :, :, pl.ds(1024 * m, 1024)].reshape((high - low) * 256, 1024)
            span = slice(256 * low, 256 * high)
            got = jnp.dot(tokens, wbuf[slot, e], preferred_element_type=F32)
            if first:
                acc[e, span, :] = got
            else:
                acc[e, span, :] += got
            return carry

        lax.fori_loop(0, 8, one, 0)

    def gate():
        names = lax.broadcasted_iota(jnp.int32, (128, 256), 0) % 64
        shares = xall[:, :, :, D:].reshape(1024, 128)

        def one(e, carry):
            pick = jnp.where(names == p.outer * 8 + e, 1.0, 0.0).astype(BF)
            scale = jnp.dot(shares, pick, preferred_element_type=F32)
            hid[:, pl.ds(pl.multiple_of(256 * e, 256), 256)] = (jnp.maximum(acc[e], 0.0) * scale).astype(BF)
            return carry

        lax.fori_loop(0, 8, one, 0)

    def run_down(m):
        def one(n, carry):
            span = pl.ds(pl.multiple_of(256 * n, 256), 256)
            weights = dbuf[m % 2, :, :, span].reshape(2048, 256)
            got = jnp.dot(hid[...], weights, preferred_element_type=F32)
            part[m, :, :, :, span] = got.astype(BF).reshape(4, 2, 128, 256)
            return carry

        lax.fori_loop(0, 4, one, 0)

    def swap(m):
        return remote(part.at[m, :, 1 - p.c], pairbuf.at[m], es.at[m], er.at[m], p.sibling())

    def give(m, d):
        return remote(part.at[m, SLOT[d], p.c], xbuf.at[m, d - 1], qs.at[m, d - 1], qr.at[m, d - 1], p.along_x(d))

    def add_pair(m):
        swap(m).wait_recv()
        for d in (1, 3, 2):
            total = part[m, SLOT[d], p.c].astype(F32) + pairbuf[m, SLOT[d]].astype(F32)
            part[m, SLOT[d], p.c] = total.astype(BF)
            give(m, d).start()

    def finish(m):
        span = pl.ds(1024 * m, 1024)
        total = hs[:, span] + part[m, 0, p.c].astype(F32) + pairbuf[m, 0].astype(F32)
        for d in (1, 3, 2):
            give(m, d).wait_recv()
            total += xbuf[m, d - 1].astype(F32)
        out[:, span] = total.astype(BF)

    def from_sibling(d):
        for h in range(2):
            across(d, h).wait_recv()

    def part_0():
        mine(1, 0).wait_recv()
        relay(1).start()
        mine(3, 1).wait_recv()
        relay(3).start()
        across(3, 0).start()
        across(1, 1).start()
        keep.wait()
        from_sibling(0)
        for m in range(3):
            land(load_up(m, m))

    def part_1():
        w.advance(3)
        mine(1, 1).wait_recv()
        across(3, 1).start()
        mine(3, 0).wait_recv()
        across(1, 0).start()
        from_sibling(1)
        from_sibling(3)
        run_up(0, 0, 0, 3, True)
        fetch(load_up(3, 0))
        run_up(1, 1, 0, 3, False)
        w.advance(4)
        run_up(2, 2, 0, 3, False)

    def part_2():
        for d in (1, 3):
            relay(d).wait_recv()
            across(2, (d - 1) // 2).start()
        land(load_up(3, 0))
        run_up(3, 0, 0, 3, False)
        w.advance(5)
        from_sibling(2)
        run_up(1, 1, 3, 4, True)
        fetch(load_up(0, 1))
        run_up(2, 2, 3, 4, False)
        w.advance(6)
        run_up(3, 0, 3, 4, False)
        load_soon(0)
        land(load_up(0, 1))
        run_up(0, 1, 3, 4, False)
        gate()

    def load_soon(m):
        w.settle(2 * m)
        w.settle(2 * m + 1)
        fetch(load_down(m))

    def produce(m):
        if m > 1:
            load_soon(m)
        if m > 0:
            add_pair(m - 1)
        if m > 1:
            finish(m - 2)
        land(load_down(m))
        run_down(m)
        swap(m).start()

    for m in range(3):
        fetch(load_up(m, m))
    w.advance(0)
    part_0()
    w.advance(2)
    part_1()
    part_2()
    w.advance(7)
    load_soon(1)
    produce(0)
    w.advance(8)
    produce(1)
    w.advance(10)
    produce(2)
    produce(3)
    add_pair(3)
    finish(2)
    finish(3)
    w.drain()
    for h in range(2):
        for d in (1, 3):
            mine(d, h).wait_send()
        for d in range(4):
            across(d, h).wait_send()
    for d in (1, 3):
        relay(d).wait_send()
    for m in range(4):
        swap(m).wait_send()
        for d in (1, 2, 3):
            give(m, d).wait_send()


def moe(ext, hidden_state, w_up, gathered_up, w_down):
    return pl.pallas_call(
        moe_kernel,
        out_shape=(
            jax.ShapeDtypeStruct((ROWS, D), BF),
            jax.ShapeDtypeStruct((8, 256, D), BF),
        ),
        in_specs=[ANY, VM, ANY, ANY, ANY],
        out_specs=(VM, ANY),
        scratch_shapes=[
            pltpu.VMEM((4, 2, ROWS, EXT), BF),
            pltpu.VMEM((8, 1024, 256), F32),
            pltpu.VMEM((1024, 2048), BF),
            pltpu.VMEM((3, 8, 1024, 256), BF),
            pltpu.VMEM((2, 8, 256, 1024), BF),
            pltpu.VMEM((4, 4, 2, ROWS, 1024), BF),
            pltpu.VMEM((4, 4, ROWS, 1024), BF),
            pltpu.VMEM((4, 3, ROWS, 1024), BF),
        ]
        + weight_sems(8)
        + [
            DMA((2, 2)), DMA((2, 2)), DMA((2,)), DMA((2,)), DMA((4, 2)), DMA((4, 2)),
            DMA((4,)), DMA((4,)), DMA((4, 3)), DMA((4, 3)), DMA((3,)), DMA((5, 4)),
        ],
        compiler_params=pltpu.CompilerParams(collective_id=3, has_side_effects=True, vmem_limit_bytes=60 * 2**20),
        name="experts",
    )(ext, hidden_state, w_up, gathered_up, w_down)[0]


def on_device(
    tokens,
    att_ids,
    mlp_ids,
    att_gain,
    att_in,
    att_router,
    att_out,
    mlp_gain,
    mlp_router,
    w_up,
    w_down,
):
    row_count = tokens.shape[0]
    chosen = jnp.any(att_ids[..., None] == jnp.arange(ATT_EXP)[None, None, None, :], axis=2)
    picked = jnp.any(mlp_ids[..., None] == jnp.arange(mlp_router.shape[1])[None, None, :], axis=1)
    ext, hidden_state, gathered_up = attention(
        tokens,
        att_gain[None, :],
        mlp_gain[None, :],
        chosen.reshape(row_count, HEADS * ATT_EXP).astype(F32),
        picked.astype(F32),
        mlp_router.T,
        att_in,
        att_router.T,
        att_out,
        w_up,
    )
    return moe(ext, hidden_state, w_up, gathered_up, w_down)


def solution(mesh):
    in_specs = (
        P(("seq", "outer", "inner"), None),
        P(("seq", "outer", "inner"), None, None),
        P(("seq", "outer", "inner"), None),
        P(),
        P("inner", None),
        P("inner", None),
        P(None, "inner"),
        P(),
        P(),
        P(("outer", "inner"), None, None),
        P(("outer", "inner"), None, None),
    )
    out_specs = P(("seq", "outer", "inner"), None)
    return jax.shard_map(
        on_device, mesh=mesh, in_specs=in_specs, out_specs=out_specs, check_vma=False
    )
```

```python
import functools

import jax
import jax.numpy as jnp
from jax import lax
from jax.experimental import pallas as pl
from jax.experimental.pallas import tpu as pltpu
from jax.sharding import PartitionSpec as P

D = 4096
HEADS = 2
HDIM = 64
ATT_EXP = 4
EXT = D + 128
ROWS = 128
SLOT = {0: 0, 1: 1, 3: 2, 2: 3}
epsilon = 1e-05
MESH = pl.DeviceIdType.MESH
ANY = pl.BlockSpec(memory_space=pl.ANY)
VM = pl.BlockSpec(memory_space=pltpu.VMEM)
DMA = pltpu.SemaphoreType.DMA
BF = jnp.bfloat16
F32 = jnp.float32


class Place:
    def __init__(self):
        self.seq, self.outer, self.inner = (lax.axis_index(a) for a in ("seq", "outer", "inner"))
        self.zl, self.y = self.seq // 4, self.seq % 4
        self.x, self.c = self.outer // 2, self.outer % 2

    def along_z(self, d):
        return (self.seq, self.outer, (self.inner + d) % 4)

    def along_y(self, d):
        return (self.zl * 4 + (self.y + d) % 4, self.outer, self.inner)

    def along_x(self, d):
        return (self.seq, ((self.x + d) % 4) * 2 + self.c, self.inner)

    def sibling(self):
        return (self.seq, self.x * 2 + 1 - self.c, self.inner)

    def pair(self):
        return ((1 - self.zl) * 4 + self.y, self.outer, self.inner)

    def beyond(self):
        return ((1 - self.zl) * 4 + self.y, self.outer, (self.inner + 2 * self.zl - 1) % 4)


def meet(peers):
    barrier = pltpu.get_barrier_semaphore()
    for peer in peers:
        pl.semaphore_signal(barrier, inc=1, device_id=peer, device_id_type=MESH)
    pl.semaphore_wait(barrier, len(peers))


def remote(src, dst, send, recv, peer):
    return pltpu.make_async_remote_copy(
        src_ref=src, dst_ref=dst, send_sem=send, recv_sem=recv, device_id=peer, device_id_type=MESH
    )


def spread_over_z(at, own, gathered, bands, p, sems):
    s1, r1, s2, r2, s3, r3, s4, r4 = sems

    def span(h, size):
        base, n, y_first = bands[h]
        outer, inner = (p.x, p.y) if y_first else (p.y, p.x)
        row = base + p.c * 16 * n + (outer * 4 * n if size < 16 else 0) + (inner * n if size < 4 else 0)
        return pl.ds(pl.multiple_of(row, n), size * n)

    def first(d, h):
        piece = span(h, 1)
        return remote(own.at[piece], gathered.at[p.inner, piece], s1.at[at, d - 1, h], r1.at[at, d - 1, h], p.along_z(d))

    def second(d, h, e):
        block = gathered.at[(p.inner - d + 4) % 4, span(h, 1)]
        peer = p.along_y(e) if bands[h][2] else p.along_x(e)
        return remote(block, block, s2.at[at, d - 1, h, e - 1], r2.at[at, d - 1, h, e - 1], peer)

    def third(d, h, e):
        block = gathered.at[(p.inner - d + 4) % 4, span(h, 4)]
        peer = p.along_x(e) if bands[h][2] else p.along_y(e)
        return remote(block, block, s3.at[at, d - 1, h, e - 1], r3.at[at, d - 1, h, e - 1], peer)

    def fourth(d, h):
        block = gathered.at[(p.inner - d + 4) % 4, span(h, 16)]
        return remote(block, block, s4.at[at, d - 1, h], r4.at[at, d - 1, h], p.sibling())

    order = (1, 3, 2)
    every = [(d, h) for d in order for h in range(len(bands))]

    def go1():
        for d, h in every:
            first(d, h).start()

    def go2():
        for d, h in every:
            first(d, h).wait_recv()
            for e in order:
                second(d, h, e).start()

    def go3():
        for d, h in every:
            for e in order:
                second(d, h, e).wait_recv()
            for e in order:
                third(d, h, e).start()

    def go4():
        for d, h in every:
            for e in order:
                third(d, h, e).wait_recv()
            fourth(d, h).start()

    def arrived():
        for d, h in every:
            fourth(d, h).wait_recv()

    def sent():
        for d, h in every:
            first(d, h).wait_send()
            fourth(d, h).wait_send()
            for e in order:
                second(d, h, e).wait_send()
                third(d, h, e).wait_send()

    return go1, go2, go3, go4, arrived, sent


def spread_sems(n):
    return [DMA((n, 3, 2))] * 2 + [DMA((n, 3, 2, 3))] * 4 + [DMA((n, 3, 2))] * 2


def square_peers(p):
    return (
        [p.along_z(d) for d in (1, 2, 3)]
        + [p.along_y(d) for d in (1, 2, 3)]
        + [p.along_x(d) for d in (1, 2, 3)]
        + [p.sibling()]
    )


class Weights:
    def __init__(self, p, steps, sems):
        self.p, self.steps = p, steps
        self.ns, self.fr, self.ps, self.sr, self.ys, self.yr = sems
        self.k = p.y % 2
        self.way = 2 * p.zl - 1
        self.done = 0

    def part(self, ref, up, e, c):
        span = pl.ds(pl.multiple_of(c * 256, 256), 256)
        return ref.at[e, span, :] if up else ref.at[e, :, span]

    def chunk(self, i, shard, c):
        _, gathered, up, _, base = self.steps[i]
        return self.part(gathered, up, ((shard + 8) % 4) * 2 + self.k, base + c)

    def to_next(self, i, t):
        p = self.p
        own, _, up, base, _ = self.steps[i]
        if t < 2:
            src = self.part(own, up, self.k, base + t)
            dst = self.chunk(i, p.inner, t)
        else:
            src = dst = self.chunk(i, p.inner - self.way, 1 - p.zl)
        return remote(src, dst, self.ns.at[i, t], self.fr.at[i, t], p.beyond())

    def far(self, t):
        p = self.p
        return (p.inner + self.way, t) if t < 2 else (p.inner + 2, p.zl)

    def near(self, t):
        p = self.p
        return (p.inner - self.way, t) if t < 2 else (p.inner + 2, 1 - p.zl)

    def forward(self, i, t):
        block = self.chunk(i, *self.far(t))
        return remote(block, block, self.ps.at[i, t], self.sr.at[i, t], self.p.pair())

    def sideways(self, i, t, which):
        shard, c = (self.far, self.near)[which](t)
        block = self.chunk(i, shard, c)
        peer = self.p.along_y(5 - 2 * (c % 2))
        return remote(block, block, self.ys.at[i, t, which], self.yr.at[i, t, which], peer)

    def begin(self, i):
        for t in range(2):
            self.to_next(i, t).start()

    def take_far(self, i, t):
        self.to_next(i, t).wait_recv()
        self.forward(i, t).start()
        self.sideways(i, t, 0).start()

    def take_near(self, i, t):
        self.forward(i, t).wait_recv()
        self.sideways(i, t, 1).start()

    def turn(self, i):
        n = len(self.steps)
        if i < n - 1:
            self.begin(i + 1)
        if i < n:
            self.take_far(i, 0)
            self.take_far(i, 1)
        if 0 <= i - 2 < n:
            self.take_far(i - 2, 2)
        if 0 <= i - 1 < n:
            self.take_near(i - 1, 0)
            self.take_near(i - 1, 1)
            self.to_next(i - 1, 2).start()
        if 0 <= i - 3 < n:
            self.take_near(i - 3, 2)

    def advance(self, to):
        for i in range(self.done, min(max(to, self.done) + 1, len(self.steps) + 3)):
            self.turn(i)
            self.done = i + 1

    def settle(self, i):
        for t in range(3):
            for which in range(2):
                self.sideways(i, t, which).wait_recv()

    def drain(self):
        for i in range(len(self.steps)):
            for t in range(3):
                self.to_next(i, t).wait_send()
                self.forward(i, t).wait_send()
                for which in range(2):
                    self.sideways(i, t, which).wait_send()

    def peers(self):
        p = self.p
        return [p.beyond(), p.pair(), p.along_y(1), p.along_y(3)]


def weight_sems(n):
    return [DMA((n, 3))] * 4 + [DMA((n, 3, 2))] * 2


def across_rows(a, b):
    return lax.dot_general(a, b, (((1,), (1,)), ((), ())), preferred_element_type=F32)


def norm_rows(src, gain, dst):
    def one(r, carry):
        rows = pl.ds(pl.multiple_of(16 * r, 16), 16)
        floats = src[rows, :].astype(F32)
        scale = lax.rsqrt(jnp.mean(floats * floats, axis=-1, keepdims=True) + epsilon)
        dst[rows, 0:D] = (floats * scale * gain[...]).astype(BF)
        return carry

    lax.fori_loop(0, 8, one, 0)


def attention_kernel(
    tok, gain, mlp_gain, chosen, picked, mlp_router, w_in, router, w_out, up, ext, hs, gup,
    normed, gw, gr, kv, gk, ao,
    s1, r1, s2, r2, s3, r3, s4, r4, ro_s, ro_r, sz, rz, sx, rx, sc, rc, local, ns, fr, ps, sr, ys, yr,
):
    p = Place()
    steps = [(up, gup, True, 2 * m, 2 * m) for m in range(8)]
    w = Weights(p, steps, (ns, fr, ps, sr, ys, yr))
    own = [
        pltpu.make_async_copy(w_in, gw.at[p.inner], local.at[0]),
        pltpu.make_async_copy(router, gr.at[p.inner], local.at[1]),
        pltpu.make_async_copy(w_out, ao.at[p.inner], local.at[2]),
    ]
    for copy in own:
        copy.start()
    meet(square_peers(p) + [p.beyond(), p.pair()])
    sems = (s1, r1, s2, r2, s3, r3, s4, r4)
    in1, in2, in3, in4, in_arrived, in_sent = spread_over_z(0, w_in, gw, ((0, 16, False), (512, 16, True)), p, sems)
    out1, out2, out3, out4, out_arrived, out_sent = spread_over_z(1, w_out, ao, ((0, 16, True),), p, sems)
    routers = [remote(router, gr.at[p.inner], ro_s.at[d - 1], ro_r.at[d - 1], p.along_z(d)) for d in (1, 2, 3)]
    zs = [remote(kv, gk.at[p.outer, p.inner], sz.at[d - 1], rz.at[d - 1], p.along_z(d)) for d in (1, 2, 3)]
    xs = [remote(gk.at[p.outer], gk.at[p.outer], sx.at[d - 1], rx.at[d - 1], p.along_x(d)) for d in (1, 2, 3)]
    cs = []
    for d in range(4):
        o = ((p.x - d + 4) % 4) * 2 + p.c
        cs.append(remote(gk.at[o], gk.at[o], sc.at[d], rc.at[d], p.sibling()))

    in1()
    for copy in routers:
        copy.start()
    w.begin(0)
    norm_rows(tok, gain, normed)
    in2()
    w.advance(0)
    in3()
    w.advance(1)
    in4()
    w.advance(2)
    in_arrived()
    for copy in routers:
        copy.wait_recv()
    own[0].wait()
    own[1].wait()

    proj = jnp.zeros((ROWS, 768), F32)
    logit = jnp.zeros((ROWS, 8), F32)
    for j in range(4):
        piece = normed[:, 1024 * j : 1024 * (j + 1)]
        proj += jnp.dot(piece, gw[j], preferred_element_type=F32)
        logit += across_rows(piece, gr[j])
    weight = jax.nn.sigmoid(logit) * chosen[...]
    mixes = []
    for h in range(HEADS):
        mix = jnp.zeros((ROWS, HDIM), F32)
        for e in range(4 * h, 4 * h + 4):
            mix += weight[:, e : e + 1] * proj[:, 256 + HDIM * e : 256 + HDIM * (e + 1)]
        mixes.append(mix)
    kv[:, 0:128] = proj[:, 128:256].astype(BF)
    kv[:, 128:256] = jnp.concatenate(mixes, axis=1).astype(BF)
    query = proj[:, 0:128].astype(BF)
    for copy in zs:
        copy.start()
    keep = pltpu.make_async_copy(kv, gk.at[p.outer, p.inner], local.at[3])
    keep.start()
    out1()
    w.advance(3)
    keep.wait()
    for copy in zs:
        copy.wait_recv()
    for copy in (xs[0], xs[2], xs[1]):
        copy.start()
    cs[0].start()
    out2()
    w.advance(4)
    out3()
    for d in (1, 3, 2):
        xs[d - 1].wait_recv()
        cs[d].start()
    w.advance(5)
    out4()
    for copy in cs:
        copy.wait_recv()

    place = (p.outer * 4 + p.inner) * ROWS + lax.broadcasted_iota(jnp.int32, (ROWS, 512), 0)
    spot = lax.broadcasted_iota(jnp.int32, (ROWS, 512), 1)
    heads = []
    for h in range(HEADS):
        mine = query[:, HDIM * h : HDIM * (h + 1)]

        def one(o, carry):
            top, total, out = carry
            held = gk[o].reshape(512, 256)
            scores = across_rows(mine, held[:, HDIM * h : HDIM * (h + 1)]) * HDIM ** (-0.5)
            scores = jnp.where(spot + 512 * o <= place, scores, -1e30)
            high = jnp.maximum(top, jnp.max(scores, axis=-1, keepdims=True))
            shares = jnp.exp(scores - high)
            fade = jnp.exp(top - high)
            values = held[:, 128 + HDIM * h : 128 + HDIM * (h + 1)]
            return (
                high,
                total * fade + jnp.sum(shares, axis=-1, keepdims=True),
                out * fade + jnp.dot(shares.astype(BF), values, preferred_element_type=F32),
            )

        start = (
            jnp.full((ROWS, 1), -1e30, F32),
            jnp.zeros((ROWS, 1), F32),
            jnp.zeros((ROWS, HDIM), F32),
        )
        _, total, out = lax.fori_loop(0, p.outer + 1, one, start)
        out = out / total
        heads.append(out * lax.rsqrt(jnp.mean(out * out, axis=-1, keepdims=True) + epsilon))
        w.advance(0)
    mixed = jnp.concatenate([weight[:, e : e + 1] * heads[e // 4] for e in range(8)], axis=1).astype(BF)
    out_arrived()
    own[2].wait()
    for j in range(4):
        span = slice(1024 * j, 1024 * (j + 1))
        hs[:, span] = tok[:, span].astype(F32) + jnp.dot(mixed, ao[j], preferred_element_type=F32)
    w.advance(0)
    norm_rows(hs, mlp_gain, ext)
    gates = jax.nn.sigmoid(across_rows(ext[:, 0:D], mlp_router[...])) * picked[...]
    high = gates.astype(BF)
    ext[:, D:] = jnp.concatenate([high, (gates - high.astype(F32)).astype(BF)], axis=1)
    w.advance(99)
    for i in range(8):
        w.settle(i)
    w.drain()
    in_sent()
    out_sent()
    for copy in routers + zs + xs + cs:
        copy.wait_send()


def attention(*arrays):
    return pl.pallas_call(
        attention_kernel,
        out_shape=(
            jax.ShapeDtypeStruct((ROWS, EXT), BF),
            jax.ShapeDtypeStruct((ROWS, D), F32),
            jax.ShapeDtypeStruct((8, D, 256), BF),
        ),
        in_specs=[VM] * 6 + [ANY] * 4,
        out_specs=(VM, VM, ANY),
        scratch_shapes=[
            pltpu.VMEM((ROWS, D), BF),
            pltpu.VMEM((4, 1024, 768), BF),
            pltpu.VMEM((4, 8, 1024), BF),
            pltpu.VMEM((ROWS, 256), BF),
            pltpu.VMEM((8, 4, ROWS, 256), BF),
            pltpu.VMEM((4, 512, 1024), BF),
        ]
        + spread_sems(2)
        + [DMA((3,))] * 6
        + [DMA((4,))] * 3
        + weight_sems(8),
        compiler_params=pltpu.CompilerParams(collective_id=1, has_side_effects=True, vmem_limit_bytes=60 * 2**20),
        name="attention",
    )(*arrays)


def moe_kernel(
    ext, hs, up, early, down, out, gdn,
    xall, acc, hid, wbuf, dbuf, part, pairbuf, xbuf,
    ns, fr, ps, sr, ys, yr, ts, tr, us, ur, vs, vr, es, er, qs, qr, local, load,
):
    p = Place()
    steps = [(down, gdn, False, 2 * m, 2 * m) for m in range(8)]
    w = Weights(p, steps, (ns, fr, ps, sr, ys, yr))
    meet(w.peers() + [p.along_x(1), p.along_x(2), p.along_x(3), p.sibling()])
    def rows(d, h):
        return xall.at[SLOT[d], p.c, pl.ds(64 * h, 64), :]

    def mine(d, h):
        src = ext.at[pl.ds(64 * h, 64), :]
        return remote(src, rows(4 - d, h), ts.at[(d - 1) // 2, h], tr.at[(d - 1) // 2, h], p.along_x(d))

    def relay(d):
        h = (d - 1) // 2
        return remote(rows(4 - d, h), rows(2, h), us.at[h], ur.at[h], p.along_x(d))

    def across(d, h):
        src = ext.at[pl.ds(64 * h, 64), :] if d == 0 else rows(d, h)
        return remote(src, rows(d, h), vs.at[d, h], vr.at[d, h], p.sibling())

    for h in range(2):
        for d in (1, 3):
            mine(d, h if d == 1 else 1 - h).start()
    for h in range(2):
        across(0, h).start()
    keep = pltpu.make_async_copy(ext, xall.at[0, p.c], local.at[2])
    keep.start()
    w.begin(0)

    def loads(own, gathered, buffer, at):
        for d in range(4):
            two = pl.ds(2 * ((p.inner + d) % 4), 2)
            src = own if d == 0 else gathered.at[two]
            yield pltpu.make_async_copy(src, buffer.at[two], load.at[at, d])

    def load_up(m, slot):
        span = pl.ds(1024 * m, 1024)
        return loads(up.at[:, span, :], early.at[:, span, :], wbuf.at[slot], slot)

    def load_down(m):
        span = pl.ds(1024 * m, 1024)
        return loads(down.at[:, :, span], gdn.at[:, :, span], dbuf.at[m % 2], 3 + m % 2)

    def fetch(copies):
        for copy in copies:
            copy.start()

    def land(copies):
        for copy in copies:
            copy.wait()

    def run_up(m, slot, low, high, first):
        def one(e, carry):
            tokens = xall[low:high, :, :, pl.ds(1024 * m, 1024)].reshape((high - low) * 256, 1024)
            span = slice(256 * low, 256 * high)
            got = jnp.dot(tokens, wbuf[slot, e], preferred_element_type=F32)
            if first:
                acc[e, span, :] = got
            else:
                acc[e, span, :] += got
            return carry

        lax.fori_loop(0, 8, one, 0)

    def gate():
        names = lax.broadcasted_iota(jnp.int32, (128, 256), 0) % 64
        shares = xall[:, :, :, D:].reshape(1024, 128)

        def one(e, carry):
            pick = jnp.where(names == p.outer * 8 + e, 1.0, 0.0).astype(BF)
            scale = jnp.dot(shares, pick, preferred_element_type=F32)
            hid[:, pl.ds(pl.multiple_of(256 * e, 256), 256)] = (jnp.maximum(acc[e], 0.0) * scale).astype(BF)
            return carry

        lax.fori_loop(0, 8, one, 0)

    def run_down(m, h):
        def one(n, carry):
            span = pl.ds(pl.multiple_of(256 * n, 256), 256)
            weights = dbuf[m % 2, :, :, span].reshape(2048, 256)
            got = jnp.dot(hid[...], weights, preferred_element_type=F32)
            part[m, :, :, :, span] = got.astype(BF).reshape(4, 2, 128, 256)
            return carry

        lax.fori_loop(2 * h, 2 * h + 2, one, 0)

    def half(h):
        return pl.ds(512 * h, 512)

    def swap(m, h):
        src = part.at[m, :, 1 - p.c, :, half(h)]
        return remote(src, pairbuf.at[m, :, :, half(h)], es.at[m, h], er.at[m, h], p.sibling())

    def give(m, h, d):
        src = part.at[m, SLOT[d], p.c, :, half(h)]
        dst = xbuf.at[m, d - 1, :, half(h)]
        return remote(src, dst, qs.at[m, h, d - 1], qr.at[m, h, d - 1], p.along_x(d))

    def add_pair(m):
        for h in range(2):
            swap(m, h).wait_recv()
            cols = slice(512 * h, 512 * (h + 1))
            for d in (2, 1, 3):
                total = part[m, SLOT[d], p.c, :, cols].astype(F32) + pairbuf[m, SLOT[d], :, cols].astype(F32)
                part[m, SLOT[d], p.c, :, cols] = total.astype(BF)
                give(m, h, d).start()

    def finish(m):
        span = pl.ds(1024 * m, 1024)
        total = hs[:, span] + part[m, 0, p.c].astype(F32) + pairbuf[m, 0].astype(F32)
        for d in (1, 3, 2):
            for h in range(2):
                give(m, h, d).wait_recv()
            total += xbuf[m, d - 1].astype(F32)
        out[:, span] = total.astype(BF)

    def from_sibling(d):
        for h in range(2):
            across(d, h).wait_recv()

    def part_0():
        mine(1, 0).wait_recv()
        relay(1).start()
        mine(3, 1).wait_recv()
        relay(3).start()
        across(3, 0).start()
        across(1, 1).start()
        keep.wait()
        from_sibling(0)
        for m in range(3):
            land(load_up(m, m))

    def part_1():
        w.advance(3)
        mine(1, 1).wait_recv()
        across(3, 1).start()
        mine(3, 0).wait_recv()
        across(1, 0).start()
        from_sibling(1)
        from_sibling(3)
        run_up(0, 0, 0, 3, True)
        fetch(load_up(3, 0))
        run_up(1, 1, 0, 3, False)
        w.advance(4)
        run_up(2, 2, 0, 3, False)

    def part_2():
        for d in (1, 3):
            relay(d).wait_recv()
            across(2, (d - 1) // 2).start()
        land(load_up(3, 0))
        run_up(3, 0, 0, 3, False)
        w.advance(5)
        from_sibling(2)
        run_up(1, 1, 3, 4, True)
        fetch(load_up(0, 1))
        run_up(2, 2, 3, 4, False)
        w.advance(6)
        run_up(3, 0, 3, 4, False)
        load_soon(0)
        land(load_up(0, 1))
        run_up(0, 1, 3, 4, False)
        gate()

    def load_soon(m):
        w.settle(2 * m)
        w.settle(2 * m + 1)
        fetch(load_down(m))

    def produce(m):
        if m > 1:
            load_soon(m)
        if m > 0:
            add_pair(m - 1)
        if m > 1:
            finish(m - 2)
        land(load_down(m))
        for h in range(2):
            run_down(m, h)
            swap(m, h).start()

    for m in range(3):
        fetch(load_up(m, m))
    w.advance(0)
    part_0()
    w.advance(2)
    part_1()
    part_2()
    w.advance(7)
    load_soon(1)
    produce(0)
    w.advance(8)
    produce(1)
    w.advance(10)
    produce(2)
    produce(3)
    add_pair(3)
    finish(2)
    finish(3)
    w.drain()
    for h in range(2):
        for d in (1, 3):
            mine(d, h).wait_send()
        for d in range(4):
            across(d, h).wait_send()
    for d in (1, 3):
        relay(d).wait_send()
    for m in range(4):
        for h in range(2):
            swap(m, h).wait_send()
            for d in (1, 2, 3):
                give(m, h, d).wait_send()


def moe(ext, hidden_state, w_up, gathered_up, w_down):
    return pl.pallas_call(
        moe_kernel,
        out_shape=(
            jax.ShapeDtypeStruct((ROWS, D), BF),
            jax.ShapeDtypeStruct((8, 256, D), BF),
        ),
        in_specs=[ANY, VM, ANY, ANY, ANY],
        out_specs=(VM, ANY),
        scratch_shapes=[
            pltpu.VMEM((4, 2, ROWS, EXT), BF),
            pltpu.VMEM((8, 1024, 256), F32),
            pltpu.VMEM((1024, 2048), BF),
            pltpu.VMEM((3, 8, 1024, 256), BF),
            pltpu.VMEM((2, 8, 256, 1024), BF),
            pltpu.VMEM((4, 4, 2, ROWS, 1024), BF),
            pltpu.VMEM((4, 4, ROWS, 1024), BF),
            pltpu.VMEM((4, 3, ROWS, 1024), BF),
        ]
        + weight_sems(8)
        + [
            DMA((2, 2)), DMA((2, 2)), DMA((2,)), DMA((2,)), DMA((4, 2)), DMA((4, 2)),
            DMA((4, 2)), DMA((4, 2)), DMA((4, 2, 3)), DMA((4, 2, 3)), DMA((3,)), DMA((5, 4)),
        ],
        compiler_params=pltpu.CompilerParams(collective_id=3, has_side_effects=True, vmem_limit_bytes=60 * 2**20),
        name="experts",
    )(ext, hidden_state, w_up, gathered_up, w_down)[0]


def on_device(
    tokens,
    att_ids,
    mlp_ids,
    att_gain,
    att_in,
    att_router,
    att_out,
    mlp_gain,
    mlp_router,
    w_up,
    w_down,
):
    row_count = tokens.shape[0]
    chosen = jnp.any(att_ids[..., None] == jnp.arange(ATT_EXP)[None, None, None, :], axis=2)
    picked = jnp.any(mlp_ids[..., None] == jnp.arange(mlp_router.shape[1])[None, None, :], axis=1)
    ext, hidden_state, gathered_up = attention(
        tokens,
        att_gain[None, :],
        mlp_gain[None, :],
        chosen.reshape(row_count, HEADS * ATT_EXP).astype(F32),
        picked.astype(F32),
        mlp_router.T,
        att_in,
        att_router.T,
        att_out,
        w_up,
    )
    return moe(ext, hidden_state, w_up, gathered_up, w_down)


def solution(mesh):
    in_specs = (
        P(("seq", "outer", "inner"), None),
        P(("seq", "outer", "inner"), None, None),
        P(("seq", "outer", "inner"), None),
        P(),
        P("inner", None),
        P("inner", None),
        P(None, "inner"),
        P(),
        P(),
        P(("outer", "inner"), None, None),
        P(("outer", "inner"), None, None),
    )
    out_specs = P(("seq", "outer", "inner"), None)
    return jax.shard_map(
        on_device, mesh=mesh, in_specs=in_specs, out_specs=out_specs, check_vma=False
    )
```
